32 devices in a mesh: rep: 4 (over x, core), dom: 8 (over z, y).
Axes of the slice: x: 2, y: 2, z: 4, core: 2. Of those that a mesh axis runs over, the one named last changes fastest.
Arguments:
- coords: float32 [4, 3, 32768], P('rep', None, 'dom'), may hold values from -6 to 6
- atom_var: float32 [32768], P('dom'), may hold values from 0.2 to 1
- atom_weight: float32 [32768], P('dom'), may hold values from 0.5 to 2
- atoms_live: int32 [256], P('dom'), may hold values from 1 to 128, 24576 in all
- block_list: int32 [256, 16], P('dom'), may hold values from 0 to 2047, as said below
- owner_map: int32 [2048], replicated, may hold values from 0 to 2047, as said below
- comp_means: float32 [3, 262144], replicated, may hold values from -6 to 6
- comp_var: float32 [262144], replicated, may hold values from 0.3 to 1.5
- comp_weight: float32 [262144], replicated, may hold values from 0.1 to 1
- target: float32 [262144], P('dom'), may hold values from 0 to 2
- noise_sigma: float32 [262144], P('dom'), may hold values from 0.05 to 0.5
Outputs:
- intersection_avg: float32 [262144], P('dom')
- forces: float32 [4, 3, 32768], P('rep', None, 'dom')
The draws below stay inside these ranges and needn't reach their ends.
Inputs may be any that keep to these rules, and one draw needn't show every extreme that they name: `atoms_live`: entry a is the number of live atoms of atom block a, held in the first slots of the block. `owner_map`: A permutation of the component blocks. Storage position p lies on dom index p // 256. `block_list`: of the 32 x 16 entries of one dom index's atom blocks, at most 64 name blocks whose storage position lies on any one dom index, and in every draw some dom index receives exactly 64 entries from every dom index. An atom block may list a component block more than once; each entry counts.
All inputs are finite; a program needn't handle non-finite values.
Results may differ from the reference program's by a relative error of at most 0.0003.
Values sent between devices are 32-bit elements; how exact they have to be, the bound alone decides.
A program may use at most 128 MiB of HBM per device.

```python
import math
import jax
import jax.numpy as jnp
import numpy as np
from jax import lax

NCOMP = 262144
ATOM_BLK = 128
COMP_BLK = 128
LISTED = 16
REPLICAS = 4
ATOMS = 32768
BLK_DEV = 32
ATOM_BLOCKS = 256
COMP_BLOCKS = 2048
CAPACITY = 64
N_DOM = 8


def owner_table(key):
    return jax.random.permutation(jax.random.fold_in(key, 11), COMP_BLOCKS).astype(jnp.int32)


def draw_owner_map(key, part):
    return owner_table(key)


def draw_block_list(key, part):
    perm = owner_table(key)
    inverse = jnp.zeros((COMP_BLOCKS,), jnp.int32).at[perm].set(jnp.arange(COMP_BLOCKS, dtype=jnp.int32))
    per_owner = COMP_BLOCKS // N_DOM
    entries = BLK_DEV * LISTED
    base = jax.random.fold_in(key, 23)
    hottest = jax.random.randint(jax.random.fold_in(base, 1), (), 0, N_DOM).astype(jnp.int32)

    def one_domain(domain_key):
        first, second, third = jax.random.split(domain_key, 3)
        pool = jax.random.permutation(first, (N_DOM - 1) * CAPACITY)[:entries - CAPACITY].astype(jnp.int32)
        others = (hottest + 1 + pool // CAPACITY) % N_DOM
        chosen = jnp.concatenate([jnp.full((CAPACITY,), hottest, jnp.int32), others])
        chosen = jax.random.permutation(second, chosen)
        inside = jax.random.randint(third, (entries,), 0, per_owner).astype(jnp.int32)
        return inverse[chosen * per_owner + inside].reshape(BLK_DEV, LISTED)
    domain_keys = jax.random.split(jax.random.fold_in(base, 2), N_DOM)
    return jax.vmap(one_domain)(domain_keys).reshape(BLK_DEV * N_DOM, LISTED).astype(jnp.int32)


def shard_levels(stream_key, dims, shards, low, high):
    def one(axis_at, blocks):
        draws = jax.random.uniform(jax.random.fold_in(jax.random.fold_in(stream_key, 6), axis_at), (blocks,), jnp.float32, low / len(shards), high / len(shards))
        return jnp.repeat(jnp.exp(draws), dims[axis_at] // blocks).reshape((-1,) + (1,) * (len(dims) - axis_at - 1))

    level = one(*shards[0])
    for cut in shards[1:]:
        level = level * one(*cut)
    return level


def split_up(count, total, reach, lean):
    loads = [(1 << 20) // math.isqrt(grade ** lean) + 1 for grade in range(2, count + 1)]
    spare, given = total - reach - (count - 1), [1] * (count - 1)
    while spare > 0:
        free = [i for i in range(count - 1) if given[i] < reach]
        mass, left = sum([loads[i] for i in free]), spare
        for i in free:
            more = min(reach - given[i], max(1, left * loads[i] // mass), spare)
            given[i] = given[i] + more
            spare = spare - more
    return np.array([reach] + given)


def uneven_parts(rng, number_of, total, limit, skew):
    if number_of == 2:
        one = jax.random.randint(rng, (), max(1, total - limit), min(limit, total - 1) + 1)
        return jnp.stack([one, total - one])
    tallies = jnp.asarray(split_up(number_of, total, limit, skew), jnp.int32)
    pairs = (number_of - 1) // 2
    source_of, receiver = tallies[1:1 + 2 * pairs:2], tallies[2:2 + 2 * pairs:2]
    room = jnp.minimum(source_of - 1, limit - receiver)
    passed = jax.random.randint(jax.random.fold_in(rng, 1), (pairs,), 0, 1 << 20) % (room + 1)
    tallies = tallies.at[1:1 + 2 * pairs:2].set(source_of - passed).at[2:2 + 2 * pairs:2].set(receiver + passed)
    return tallies[jax.random.permutation(jax.random.fold_in(rng, 2), number_of)]


def normal_values(key, dims, deviation, bound, pieces=(), held_as=jnp.bfloat16):
    drawn = deviation * jax.random.normal(key, dims, jnp.float32)
    if pieces:
        drawn = drawn * shard_levels(key, dims, pieces, -0.22, 0.18)
    return jnp.clip(drawn, -bound, bound).astype(held_as)


def setup_inputs(seed: int = 0) -> dict:
    key_list = jax.random.split(jax.random.key(seed), 12)
    return {
        "coords": normal_values(key_list[0], (REPLICAS, 3, ATOMS), 1.0, 6.0, ((0, 4), (2, 8)), jnp.float32),
        "atom_var": jnp.clip(jnp.exp(math.log(1.0) - 1.609438 * jax.random.uniform(key_list[1], (ATOMS,), jnp.float32) ** shard_levels(key_list[1], (ATOMS,), ((0, 8),), -0.2, 0.2)), 0.2, 1.0),
        "atom_weight": jnp.clip(0.5 + 1.5 * jax.random.uniform(key_list[2], (ATOMS,), jnp.float32) ** shard_levels(key_list[2], (ATOMS,), ((0, 8),), -0.2, 0.2), 0.5, 2.0),
        "atoms_live": uneven_parts(key_list[3], ATOM_BLOCKS, ATOM_BLOCKS * ATOM_BLK * 3 // 4, ATOM_BLK, 0).astype(jnp.int32),
        "block_list": draw_block_list(jax.random.fold_in(key_list[11], 71), 0),
        "owner_map": draw_owner_map(jax.random.fold_in(key_list[11], 71), 0),
        "comp_means": normal_values(key_list[6], (3, NCOMP), 1.0, 6.0, (), jnp.float32),
        "comp_var": jnp.clip(jnp.exp(jax.random.uniform(key_list[7], (NCOMP,), jnp.float32, math.log(0.3), math.log(1.5))), 0.3, 1.5),
        "comp_weight": jnp.clip(jnp.exp(jax.random.uniform(key_list[8], (NCOMP,), jnp.float32, math.log(0.1), math.log(1.0))), 0.1, 1.0),
        "target": jnp.clip(2.0 * jax.random.uniform(key_list[9], (NCOMP,), jnp.float32) ** shard_levels(key_list[9], (NCOMP,), ((0, 8),), -0.2, 0.2), 0.0, 2.0),
        "noise_sigma": jnp.clip(jnp.exp(math.log(0.5) - 2.3025851 * jax.random.uniform(key_list[10], (NCOMP,), jnp.float32) ** shard_levels(key_list[10], (NCOMP,), ((0, 8),), -0.2, 0.2)), 0.05, 0.5),
    }


full_turn = 2.0 * math.pi
energy_unit = 2.494


def intersection_tile(positions, variances, weights, centers, center_var, center_weight):
    offsets = positions[:, None, :, None] - centers[:, :, None, :]
    squared = jnp.sum(offsets * offsets, axis=0)
    widths = variances[None, :, None] + center_var[:, None, :]
    prefactor = weights[None, :, None] * center_weight[:, None, :]
    intersection = prefactor * (full_turn * widths) ** -1.5 * jnp.exp(-0.5 * squared / widths)
    return offsets, widths, intersection


def reference(coords, atom_var, atom_weight, atoms_live, block_list, owner_map, comp_means, comp_var, comp_weight, target, noise_sigma):
    blocks = block_list.shape[0]
    replicas = coords.shape[0]
    slot_index = jnp.arange(ATOM_BLK, dtype=jnp.int32)
    live_mask = (slot_index[None, :] < atoms_live[:, None]).astype(atom_weight.dtype)
    positions = coords.reshape(replicas, 3, blocks, ATOM_BLK).transpose(2, 0, 1, 3)
    variances = atom_var.reshape(blocks, ATOM_BLK)
    weights = atom_weight.reshape(blocks, ATOM_BLK) * live_mask
    centers = comp_means.reshape(3, COMP_BLOCKS, COMP_BLK)
    center_var = comp_var.reshape(COMP_BLOCKS, COMP_BLK)
    center_weight = comp_weight.reshape(COMP_BLOCKS, COMP_BLK)
    tiled = jax.vmap(intersection_tile, in_axes=(0, None, None, None, None, None))

    def partial_of(inputs):
        coord_tile, var_tile, weight_tile, blocks_of = inputs
        offsets, widths, intersection = tiled(coord_tile, var_tile, weight_tile, centers[:, blocks_of], center_var[blocks_of], center_weight[blocks_of])
        return jnp.sum(intersection, axis=2)

    inputs = (positions, variances, weights, block_list)
    partials = lax.map(partial_of, inputs)
    flattened = partials.transpose(0, 2, 1, 3).reshape(blocks * LISTED, replicas, COMP_BLK)
    summed = jax.ops.segment_sum(flattened, block_list.reshape(-1), num_segments=COMP_BLOCKS)
    mean_logical = jnp.sum(summed, axis=1) / replicas
    intersection_avg = jnp.zeros_like(mean_logical).at[owner_map].set(mean_logical).reshape(-1)
    wanted = target.reshape(COMP_BLOCKS, COMP_BLK)[owner_map]
    sigmas = noise_sigma.reshape(COMP_BLOCKS, COMP_BLK)[owner_map]
    misfit = mean_logical - wanted
    adjoint = misfit / (sigmas * sigmas + 0.5 * misfit * misfit) / replicas

    def force_of(inputs):
        coord_tile, var_tile, weight_tile, blocks_of = inputs
        offsets, widths, intersection = tiled(coord_tile, var_tile, weight_tile, centers[:, blocks_of], center_var[blocks_of], center_weight[blocks_of])
        weight = adjoint[blocks_of][None, :, None, :] * (intersection / widths)
        return energy_unit * jnp.sum(weight[:, None] * offsets, axis=(2, 4))

    forces = lax.map(force_of, inputs)
    forces = forces.transpose(1, 2, 0, 3).reshape(replicas, 3, blocks * ATOM_BLK)
    return intersection_avg, forces
```

```python
import functools
import math

import jax
import jax.numpy as jnp
from jax import lax
from jax.experimental import pallas as pl
from jax.experimental.pallas import tpu as pltpu
from jax.sharding import PartitionSpec as P

CAPACITY = 64
LANES = 128
STRIP = 16
ROWS = 64

energy_unit = 2.494
norm = (2.0 * math.pi) ** -1.5
half_log2e = -0.5 / math.log(2.0)
dead = -1.0e4
VMEM = pltpu.VMEM
SMEM = pltpu.SMEM
MESH = pl.DeviceIdType.MESH
f32, i32, bf16 = jnp.float32, jnp.int32, jnp.bfloat16


def split(value):
    second = value - value.astype(bf16).astype(f32)
    third = second - second.astype(bf16).astype(f32)
    return value, second, third


def pieces_of(value):
    return [piece.astype(bf16) for piece in split(value)]


def dot3(picks, value):
    total = None
    for piece in pieces_of(value):
        part = jnp.dot(picks, piece, preferred_element_type=f32)
        total = part if total is None else total + part
    return total


def iota(shape, axis):
    return lax.broadcasted_iota(i32, shape, axis)


def splat_rows(tile):
    return jnp.transpose(tile)


def step_kernel(
    replicas, domains, blocks, listed, owned,
    live_h, lst_h, owner_h, x_h, av_h, aw_h, m_h, cv_h, cw_h, target_h, sigma_h,
    f_ref, mean_ref,
    live, lst, owner, x_v, av_v, aw_v, m_v, cv_v, cw_v, target_v, sigma_v,
    g_v, lhs_s, avt_s, rhs_s, part, dev_s, slot_s, perm_a, perm_b, slot_send, slot_land,
    out_send, out_land, back_send, back_land, ret, adj_e, mean_send, mean_land, sums,
    loads, slot_ss, slot_rs, out_ss, out_rs, back_ss, back_rs, mean_ss, mean_rs,
):
    me_r = lax.axis_index("rep")
    me_d = lax.axis_index("dom")
    entries = blocks * listed
    slots = domains * CAPACITY
    width = LANES // replicas
    slab = CAPACITY // replicas
    per = LANES // CAPACITY
    devices = replicas * domains
    chunk = owned // replicas
    fetches = [
        pltpu.make_async_copy(src, dst, loads.at[i])
        for i, (src, dst) in enumerate(
            [(lst_h, lst), (owner_h, owner), (live_h, live), (x_h, x_v), (av_h, av_v), (aw_h, aw_v),
             (m_h, m_v), (cv_h, cv_v), (cw_h, cw_v), (target_h, target_v), (sigma_h, sigma_v)]
        )
    ]
    for fetch in fetches:
        fetch.start()
    barrier = pltpu.get_barrier_semaphore()

    def peer(s):
        return lax.rem(me_r + s // domains, replicas), lax.rem(me_d + lax.rem(s, domains), domains)

    def greet(s, carry):
        pl.semaphore_signal(barrier, inc=1, device_id=peer(s), device_id_type=MESH)
        return carry

    lax.fori_loop(1, devices, greet, 0)
    for fetch in fetches[:6]:
        fetch.wait()

    lane = iota((1, LANES), 1)
    group = lane // width
    one = jnp.ones((1, LANES), f32)
    zero = jnp.zeros((1, LANES), f32)

    def places(a, carry):
        for k in range(listed):
            place = owner[lst[k, a]]
            dev = lax.div(place, owned)
            e = a * listed + k
            dev_s[pl.ds(e, 1), :] = jnp.full((1, LANES), dev, i32)
            slot_s[pl.ds(e, 1), :] = jnp.full((1, LANES), place - dev * owned + 1, i32)
        return carry

    lax.fori_loop(0, blocks, places, 0)
    dev = dev_s[...]
    hot = jnp.where(dev == lane, 1.0, 0.0)
    before = jnp.where(iota((entries, entries), 1) < iota((entries, entries), 0), 1.0, 0.0).astype(bf16)
    rank = jnp.dot(before, hot.astype(bf16), preferred_element_type=f32)
    rank = jnp.sum(rank * hot, axis=1, keepdims=True)
    place = dev * CAPACITY + jnp.broadcast_to(rank, (entries, LANES)).astype(i32)
    for j in range(slots // LANES):
        perm_b[:, j * LANES : (j + 1) * LANES] = jnp.where(place == lane + j * LANES, 1.0, 0.0).astype(bf16)
    place_f = place.astype(f32)
    for j in range(entries // LANES):
        row = jnp.transpose(place_f[j * LANES : (j + 1) * LANES])[0:1].astype(i32)
        perm_a[:, j * LANES : (j + 1) * LANES] = jnp.where(
            iota((slots, LANES), 0) == row, 1.0, 0.0
        ).astype(bf16)
    slot_c = jnp.dot(perm_a[...], slot_s[...].astype(f32).astype(bf16), preferred_element_type=f32)
    for j in range(slots // LANES):
        slot_send[j] = jnp.transpose(slot_c[j * LANES : (j + 1) * LANES])[0:8]
    pl.semaphore_wait(barrier, devices - 1)

    def slot_copy(s):
        to = lax.rem(me_d + s, domains)
        return pltpu.make_async_remote_copy(
            src_ref=slot_send.at[to // per], dst_ref=slot_land.at[s],
            send_sem=slot_ss.at[s], recv_sem=slot_rs.at[s],
            device_id=(me_r, to), device_id_type=MESH,
        )

    for s in range(1, domains):
        slot_copy(s).start()
    slot_land[0] = slot_send[me_d // per]

    for fetch in fetches[6:]:
        fetch.wait()
    none = jnp.zeros((8, LANES), f32)

    def prepare(a):
        turn = lax.rem(a, 2)
        x = jnp.concatenate(
            [x_v[c, :, pl.ds(pl.multiple_of(a * LANES, LANES), LANES)] for c in range(3)], axis=0
        )
        xx = jnp.sum(x * x, axis=0, keepdims=True)
        av = av_v[pl.ds(a, 1), :]
        lw = jnp.where(lane < live[a], jnp.log2(aw_v[pl.ds(a, 1), :]), dead)
        left = jnp.concatenate(
            [half_log2e * -2.0 * x, half_log2e * one, half_log2e * xx + av * lw, lw, zero, zero], axis=0
        )
        l0, l1, l2 = split(left)
        big = jnp.concatenate([l0, l0, l1, l1, l0, l2, none, none], axis=0)
        lhs_s[turn] = jnp.transpose(big.astype(bf16))
        avt_s[turn] = jnp.transpose(jnp.broadcast_to(av, (LANES, LANES)))
        for k in range(listed):
            b = lst[k, a]
            m = m_v[b]
            mm = jnp.sum(m * m, axis=0, keepdims=True)
            r0, r1, r2 = split(jnp.concatenate([m, mm, one, cv_v[b], zero, zero], axis=0))
            here = slice((k % 2) * LANES, (k % 2 + 1) * LANES)
            rhs_s[turn, k // 2, 0:16, here] = jnp.concatenate([r0, r1], axis=0).astype(bf16)
            rhs_s[turn, k // 2, 16:32, here] = jnp.concatenate([r2, r0], axis=0).astype(bf16)

    blank = jnp.zeros((16, 2 * LANES), bf16)

    def pairs(a, carry):
        turn = lax.rem(a, 2)
        lhs = lhs_s[turn]
        for k in range(0, listed, 2):
            upper, lower = rhs_s[turn, k // 2, 0:16], rhs_s[turn, k // 2, 16:32]
            rhs = jnp.concatenate([upper, upper, lower, blank], axis=0)
            scaled = jnp.dot(lhs, rhs, preferred_element_type=f32)
            for i in range(2):
                e = a * listed + k + i
                b = lst[k + i, a]
                cv = jnp.broadcast_to(cv_v[b], (8, LANES))
                total = jnp.zeros((8, LANES), f32)
                for h in range(0, LANES, 8):
                    root = lax.rsqrt(avt_s[turn, h : h + 8, :] + cv)
                    inv = root * root
                    ov = (root * inv) * jnp.exp2(scaled[h : h + 8, i * LANES : (i + 1) * LANES] * inv)
                    total = total + ov
                    g_v[e, h : h + 8, :] = ov * inv
                part[pl.ds(e, 1), :] = jnp.sum(total, axis=0, keepdims=True) * (norm * cw_v[b])
        prepare(lax.rem(a + 1, blocks))
        return carry

    prepare(0)
    lax.fori_loop(0, blocks, pairs, 0)

    def turned(pieces, to):
        total = None
        for g in range(replicas):
            shift = (width * (g - to)) % LANES
            piece = pltpu.roll(pieces[g], shift, axis=1) if shift else pieces[g]
            piece = jnp.where(group == g, piece, 0.0)
            total = piece if total is None else total + piece
        return total

    def fold(value):
        shift = width
        while shift < LANES:
            value = value + pltpu.roll(value, shift, axis=1)
            shift = 2 * shift
        return value

    placed = dot3(perm_a[...], part[...]).reshape(domains, replicas, slab, LANES)
    parts = [placed[:, g].reshape(domains * slab, LANES) for g in range(replicas)]
    for q in range(replicas):
        out_send[q] = turned(parts, q).reshape(domains, slab, LANES)

    def out_copy(s):
        to_r, to_d = peer(s)
        return pltpu.make_async_remote_copy(
            src_ref=out_send.at[to_r, to_d], dst_ref=out_land.at[s],
            send_sem=out_ss.at[s], recv_sem=out_rs.at[s],
            device_id=(to_r, to_d), device_id_type=MESH,
        )

    def start_out(s, carry):
        out_copy(s).start()
        return carry

    lax.fori_loop(1, devices, start_out, 0)
    out_land[0] = out_send[me_r, me_d]

    mine = group == me_r
    wanted = fold(jnp.where(mine, target_v[...], 0.0))
    sigmas = fold(jnp.where(mine, sigma_v[...], 0.0))
    for s in range(1, domains):
        slot_copy(s).wait_recv()
    odd = lax.rem(me_d, per)
    rows = []
    for j in range(domains // per):
        total = None
        for i in range(per):
            tile = slot_land[j * per + i]
            moved = None
            for n in range(per):
                shift = ((i - n) * CAPACITY) % LANES
                option = pltpu.roll(tile, shift, axis=1) if shift else tile
                moved = option if moved is None else jnp.where(odd == n, option, moved)
            moved = jnp.where(lane // CAPACITY == i, moved, 0.0)
            total = moved if total is None else total + moved
        rows.append(total[0:1].astype(i32))
    picks = jnp.concatenate(
        [jnp.where(iota((owned, LANES), 0) + 1 == row, 1.0, 0.0).astype(bf16) for row in rows], axis=1
    )

    def wait_out(s, carry):
        out_copy(s).wait_recv()
        return carry

    lax.fori_loop(1, devices, wait_out, 0)
    spread = []
    for s in range(domains):
        total = out_land[s]
        for r in range(1, replicas):
            total = total + out_land[r * domains + s]
        for g in range(replicas):
            spread.append(jnp.where(group == g, total, 0.0))
    mean = fold(dot3(picks, jnp.concatenate(spread, axis=0))) / replicas
    misfit = mean - wanted
    adjoint = misfit / (sigmas * sigmas + 0.5 * misfit * misfit) / replicas
    adjoints = pieces_of(adjoint)
    for s in range(domains):
        value = None
        for piece in adjoints:
            one_part = lax.dot_general(
                picks[:, (s // per) * LANES : (s // per + 1) * LANES], piece,
                (((0,), (0,)), ((), ())), preferred_element_type=f32,
            )[(s % per) * CAPACITY : (s % per + 1) * CAPACITY]
            value = one_part if value is None else value + one_part
        packed = None
        for g in range(replicas):
            piece = jnp.where(group == g, value[g * slab : (g + 1) * slab], 0.0)
            packed = piece if packed is None else packed + piece
        back_send[s] = packed

    def back_copy(n):
        s = lax.rem(n, domains)
        to = lax.rem(me_r + n // domains, replicas), lax.rem(me_d + domains - s, domains)
        return pltpu.make_async_remote_copy(
            src_ref=back_send.at[s], dst_ref=back_land.at[n],
            send_sem=back_ss.at[n], recv_sem=back_rs.at[n],
            device_id=to, device_id_type=MESH,
        )

    def start_back(n, carry):
        back_copy(n).start()
        return carry

    lax.fori_loop(1, devices, start_back, 0)
    back_land[0] = back_send[0]
    packed = None
    for g in range(replicas):
        piece = jnp.where(group == g, mean[g * chunk : (g + 1) * chunk], 0.0)
        packed = piece if packed is None else packed + piece
    mean_send[...] = packed

    def mean_copy(n):
        return pltpu.make_async_remote_copy(
            src_ref=mean_send, dst_ref=mean_land.at[n],
            send_sem=mean_ss.at[n], recv_sem=mean_rs.at[n],
            device_id=(lax.rem(me_r + n, replicas), me_d), device_id_type=MESH,
        )

    for n in range(1, replicas):
        mean_copy(n).start()
    mean_land[0] = packed

    def wait_back(n, carry):
        back_copy(n).wait_recv()
        return carry

    lax.fori_loop(1, devices, wait_back, 0)
    source = [lax.rem(me_r + replicas - q, replicas) for q in range(replicas)]
    for s in range(domains):
        messages = [back_land[source[q] * domains + s] for q in range(replicas)]
        ret[lax.rem(me_d + s, domains)] = jnp.concatenate(
            [turned(messages, g) for g in range(replicas)], axis=0
        )
    adj_e[...] = dot3(perm_b[...], ret[...].reshape(slots, LANES))
    ones = jnp.ones((8, LANES), f32)

    def forces(a, carry):
        coefs = []
        for k in range(listed):
            b = lst[k, a]
            scale = (energy_unit * norm) * cw_v[b] * adj_e[pl.ds(a * listed + k, 1), :]
            m = m_v[b]
            sums[4, k * 4 : k * 4 + 4, :] = jnp.concatenate([scale, m * scale], axis=0)
        for h in range(0, LANES, STRIP):
            acc = [[jnp.zeros((8, LANES), f32) for _ in range(STRIP // 8)] for _ in range(4)]
            for k in range(listed):
                rows = [
                    jnp.broadcast_to(sums[4, k * 4 + c : k * 4 + c + 1, :], (8, LANES)) for c in range(4)
                ]
                for q in range(STRIP // 8):
                    g = g_v[a * listed + k, h + q * 8 : h + q * 8 + 8, :]
                    for c in range(4):
                        acc[c][q] = acc[c][q] + g * rows[c]
            for c in range(4):
                for q in range(STRIP // 8):
                    sums[c, h + q * 8 : h + q * 8 + 8, :] = acc[c][q]
        flat = [
            lax.dot_general(
                ones, sums[c], (((1,), (1,)), ((), ())), precision=lax.Precision.HIGHEST,
                preferred_element_type=f32,
            )[0:1]
            for c in range(4)
        ]
        here = pl.ds(pl.multiple_of(a * LANES, LANES), LANES)
        for c in range(3):
            f_ref[c, :, here] = x_v[c, :, here] * flat[0] - flat[c + 1]
        return carry

    lax.fori_loop(0, blocks, forces, 0)
    for n in range(1, replicas):
        mean_copy(n).wait_recv()
    messages = [mean_land[source[q]] for q in range(replicas)]
    for g in range(replicas):
        mean_ref[g * chunk : (g + 1) * chunk, :] = turned(messages, g)

    def sent(s, carry):
        out_copy(s).wait_send()
        back_copy(s).wait_send()
        return carry

    lax.fori_loop(1, devices, sent, 0)
    for s in range(1, domains):
        slot_copy(s).wait_send()
    for n in range(1, replicas):
        mean_copy(n).wait_send()


def shards(
    coords, atom_var, atom_weight, atoms_live, block_list, owner_map,
    comp_means, comp_var, comp_weight, target, noise_sigma,
):
    replicas = lax.axis_size("rep")
    domains = lax.axis_size("dom")
    blocks, listed = block_list.shape
    comp_blocks = owner_map.shape[0]
    owned = target.shape[0] // LANES
    entries = blocks * listed
    slots = domains * CAPACITY
    devices = domains * replicas
    slab = CAPACITY // replicas
    per = LANES // CAPACITY
    x = coords.transpose(1, 0, 2)
    cm = comp_means.reshape(3, comp_blocks, LANES).transpose(1, 0, 2)
    cv = comp_var.reshape(comp_blocks, 1, LANES)
    cw = comp_weight.reshape(comp_blocks, 1, LANES)
    whole = pl.BlockSpec(memory_space=VMEM)
    far = pl.BlockSpec(memory_space=pltpu.HBM)
    dma = pltpu.SemaphoreType.DMA
    forces, mean = pl.pallas_call(
        functools.partial(step_kernel, replicas, domains, blocks, listed, owned),
        in_specs=[far] * 11,
        out_specs=[whole] * 2,
        out_shape=[
            jax.ShapeDtypeStruct(x.shape, f32),
            jax.ShapeDtypeStruct((owned, LANES), f32),
        ],
        scratch_shapes=[
            SMEM((blocks,), i32),
            SMEM((listed, blocks), i32),
            SMEM((comp_blocks,), i32),
            VMEM(x.shape, f32),
            VMEM((blocks, LANES), f32),
            VMEM((blocks, LANES), f32),
            VMEM(cm.shape, f32),
            VMEM(cv.shape, f32),
            VMEM(cw.shape, f32),
            VMEM((owned, LANES), f32),
            VMEM((owned, LANES), f32),
            VMEM((entries, LANES, LANES), f32),
            VMEM((2, LANES, ROWS), bf16),
            VMEM((2, LANES, LANES), f32),
            VMEM((2, listed // 2, 32, 2 * LANES), bf16),
            VMEM((entries, LANES), f32),
            VMEM((entries, LANES), i32),
            VMEM((entries, LANES), i32),
            VMEM((slots, entries), bf16),
            VMEM((entries, slots), bf16),
            VMEM((slots // LANES, 8, LANES), f32),
            VMEM((domains, 8, LANES), f32),
            VMEM((replicas, domains, slab, LANES), f32),
            VMEM((devices, slab, LANES), f32),
            VMEM((domains, slab, LANES), f32),
            VMEM((devices, slab, LANES), f32),
            VMEM((domains, CAPACITY, LANES), f32),
            VMEM((entries, LANES), f32),
            VMEM((owned // replicas, LANES), f32),
            VMEM((replicas, owned // replicas, LANES), f32),
            VMEM((5, LANES, LANES), f32),
            dma((11,)),
            dma((domains,)),
            dma((domains,)),
            dma((devices,)),
            dma((devices,)),
            dma((devices,)),
            dma((devices,)),
            dma((replicas,)),
            dma((replicas,)),
        ],
        compiler_params=pltpu.CompilerParams(
            collective_id=0, has_side_effects=True, vmem_limit_bytes=60 << 20
        ),
        name="step",
    )(
        atoms_live, block_list.T, owner_map, x,
        atom_var.reshape(blocks, LANES), atom_weight.reshape(blocks, LANES),
        cm, cv, cw, target.reshape(owned, LANES), noise_sigma.reshape(owned, LANES),
    )
    return (mean.reshape(-1), forces.transpose(1, 0, 2))


def solution(mesh):
    return jax.shard_map(
        shards,
        mesh=mesh,
        in_specs=(
            P("rep", None, "dom"),
            P("dom"),
            P("dom"),
            P("dom"),
            P("dom", None),
            P(),
            P(),
            P(),
            P(),
            P("dom"),
            P("dom"),
        ),
        out_specs=(P("dom"), P("rep", None, "dom")),
        check_vma=False,
    )
```

```python
import functools
import math

import jax
import jax.numpy as jnp
from jax import lax
from jax.experimental import pallas as pl
from jax.experimental.pallas import tpu as pltpu
from jax.sharding import PartitionSpec as P

CAPACITY = 64
LANES = 128
STRIP = 16
ROWS = 64

energy_unit = 2.494
norm = (2.0 * math.pi) ** -1.5
half_log2e = -0.5 / math.log(2.0)
dead = -1.0e4
VMEM = pltpu.VMEM
SMEM = pltpu.SMEM
MESH = pl.DeviceIdType.MESH
f32, i32, bf16 = jnp.float32, jnp.int32, jnp.bfloat16


def split(value):
    second = value - value.astype(bf16).astype(f32)
    third = second - second.astype(bf16).astype(f32)
    return value, second, third


def pieces_of(value):
    return [piece.astype(bf16) for piece in split(value)]


def dot3(picks, value):
    total = None
    for piece in pieces_of(value):
        part = jnp.dot(picks, piece, preferred_element_type=f32)
        total = part if total is None else total + part
    return total


def iota(shape, axis):
    return lax.broadcasted_iota(i32, shape, axis)


def step_kernel(
    replicas, domains, blocks, listed, owned,
    live_h, lst_h, owner_h, x_h, av_h, aw_h, m_h, cv_h, cw_h, target_h, sigma_h,
    f_ref, mean_ref,
    live, lst, owner, x_v, av_v, aw_v, m_v, cv_v, cw_v, target_v, sigma_v,
    g_v, lhs_s, avt_s, rhs_s, part, dev_s, slot_s, perm_a, perm_b, slot_send, slot_land,
    out_send, out_land, back_send, back_land, ret, adj_e, mean_send, mean_land, sums, coefs,
    loads, slot_ss, slot_rs, out_ss, out_rs, back_ss, back_rs, mean_ss, mean_rs,
):
    me_r = lax.axis_index("rep")
    me_d = lax.axis_index("dom")
    entries = blocks * listed
    slots = domains * CAPACITY
    width = LANES // replicas
    slab = CAPACITY // replicas
    per = LANES // CAPACITY
    devices = replicas * domains
    chunk = owned // replicas
    fetches = [
        pltpu.make_async_copy(src, dst, loads.at[i])
        for i, (src, dst) in enumerate(
            [(lst_h, lst), (owner_h, owner), (live_h, live), (x_h, x_v), (av_h, av_v), (aw_h, aw_v),
             (m_h, m_v), (cv_h, cv_v), (cw_h, cw_v), (target_h, target_v), (sigma_h, sigma_v)]
        )
    ]
    for fetch in fetches:
        fetch.start()
    barrier = pltpu.get_barrier_semaphore()

    def peer(s):
        return lax.rem(me_r + s // domains, replicas), lax.rem(me_d + lax.rem(s, domains), domains)

    def greet(s, carry):
        pl.semaphore_signal(barrier, inc=1, device_id=peer(s), device_id_type=MESH)
        return carry

    lax.fori_loop(1, devices, greet, 0)
    for fetch in fetches[:6]:
        fetch.wait()

    lane = iota((1, LANES), 1)
    group = lane // width
    one = jnp.ones((1, LANES), f32)
    zero = jnp.zeros((1, LANES), f32)

    def places(a, carry):
        for k in range(listed):
            place = owner[lst[k, a]]
            dev = lax.div(place, owned)
            e = a * listed + k
            dev_s[pl.ds(e, 1), :] = jnp.full((1, LANES), dev, i32)
            slot_s[pl.ds(e, 1), :] = jnp.full((1, LANES), place - dev * owned + 1, i32)
        return carry

    lax.fori_loop(0, blocks, places, 0)
    dev = dev_s[...]
    hot = jnp.where(dev == lane, 1.0, 0.0)
    before = jnp.where(iota((entries, entries), 1) < iota((entries, entries), 0), 1.0, 0.0).astype(bf16)
    rank = jnp.dot(before, hot.astype(bf16), preferred_element_type=f32)
    rank = jnp.sum(rank * hot, axis=1, keepdims=True)
    place = dev * CAPACITY + jnp.broadcast_to(rank, (entries, LANES)).astype(i32)
    for j in range(slots // LANES):
        perm_b[:, j * LANES : (j + 1) * LANES] = jnp.where(place == lane + j * LANES, 1.0, 0.0).astype(bf16)
    place_f = place.astype(f32)
    for j in range(entries // LANES):
        row = jnp.transpose(place_f[j * LANES : (j + 1) * LANES])[0:1].astype(i32)
        perm_a[:, j * LANES : (j + 1) * LANES] = jnp.where(
            iota((slots, LANES), 0) == row, 1.0, 0.0
        ).astype(bf16)
    slot_c = jnp.dot(perm_a[...], slot_s[...].astype(f32).astype(bf16), preferred_element_type=f32)
    for j in range(slots // LANES):
        slot_send[j] = jnp.transpose(slot_c[j * LANES : (j + 1) * LANES])[0:8]
    pl.semaphore_wait(barrier, devices - 1)

    def slot_copy(s):
        to = lax.rem(me_d + s, domains)
        return pltpu.make_async_remote_copy(
            src_ref=slot_send.at[to // per], dst_ref=slot_land.at[s],
            send_sem=slot_ss.at[s], recv_sem=slot_rs.at[s],
            device_id=(me_r, to), device_id_type=MESH,
        )

    for s in range(1, domains):
        slot_copy(s).start()
    slot_land[0] = slot_send[me_d // per]

    for fetch in fetches[6:]:
        fetch.wait()
    none = jnp.zeros((8, LANES), f32)

    def prepare(a):
        turn = lax.rem(a, 2)
        x = jnp.concatenate(
            [x_v[c, :, pl.ds(pl.multiple_of(a * LANES, LANES), LANES)] for c in range(3)], axis=0
        )
        xx = jnp.sum(x * x, axis=0, keepdims=True)
        av = av_v[pl.ds(a, 1), :]
        lw = jnp.where(lane < live[a], jnp.log2(aw_v[pl.ds(a, 1), :]), dead)
        left = jnp.concatenate(
            [half_log2e * -2.0 * x, half_log2e * one, half_log2e * xx + av * lw, lw, zero, zero], axis=0
        )
        l0, l1, l2 = split(left)
        big = jnp.concatenate([l0, l0, l1, l1, l0, l2, none, none], axis=0)
        lhs_s[turn] = jnp.transpose(big.astype(bf16))
        avt_s[turn] = jnp.transpose(jnp.broadcast_to(av, (LANES, LANES)))
        for k in range(listed):
            b = lst[k, a]
            m = m_v[b]
            mm = jnp.sum(m * m, axis=0, keepdims=True)
            r0, r1, r2 = split(jnp.concatenate([m, mm, one, cv_v[b], zero, zero], axis=0))
            here = slice((k % 2) * LANES, (k % 2 + 1) * LANES)
            rhs_s[turn, k // 2, 0:16, here] = jnp.concatenate([r0, r1], axis=0).astype(bf16)
            rhs_s[turn, k // 2, 16:32, here] = jnp.concatenate([r2, r0], axis=0).astype(bf16)

    blank = jnp.zeros((16, 2 * LANES), bf16)

    def pairs(a, carry):
        turn = lax.rem(a, 2)
        lhs = lhs_s[turn]
        for k in range(0, listed, 2):
            upper, lower = rhs_s[turn, k // 2, 0:16], rhs_s[turn, k // 2, 16:32]
            rhs = jnp.concatenate([upper, upper, lower, blank], axis=0)
            scaled = jnp.dot(lhs, rhs, preferred_element_type=f32)
            for i in range(2):
                e = a * listed + k + i
                b = lst[k + i, a]
                cv = jnp.broadcast_to(cv_v[b], (8, LANES))
                total = jnp.zeros((8, LANES), f32)
                for h in range(0, LANES, 8):
                    root = lax.rsqrt(avt_s[turn, h : h + 8, :] + cv)
                    inv = root * root
                    ov = (root * inv) * jnp.exp2(scaled[h : h + 8, i * LANES : (i + 1) * LANES] * inv)
                    total = total + ov
                    g_v[e, h : h + 8, :] = ov * inv
                part[pl.ds(e, 1), :] = jnp.sum(total, axis=0, keepdims=True) * (norm * cw_v[b])
        prepare(lax.rem(a + 1, blocks))
        return carry

    prepare(0)
    lax.fori_loop(0, blocks, pairs, 0)

    def turned(pieces, to):
        total = None
        for g in range(replicas):
            shift = (width * (g - to)) % LANES
            piece = pltpu.roll(pieces[g], shift, axis=1) if shift else pieces[g]
            piece = jnp.where(group == g, piece, 0.0)
            total = piece if total is None else total + piece
        return total

    def fold(value):
        shift = width
        while shift < LANES:
            value = value + pltpu.roll(value, shift, axis=1)
            shift = 2 * shift
        return value

    placed = dot3(perm_a[...], part[...]).reshape(domains, replicas, slab, LANES)
    parts = [placed[:, g].reshape(domains * slab, LANES) for g in range(replicas)]
    for q in range(replicas):
        out_send[q] = turned(parts, q).reshape(domains, slab, LANES)

    def out_copy(s):
        to_r, to_d = peer(s)
        return pltpu.make_async_remote_copy(
            src_ref=out_send.at[to_r, to_d], dst_ref=out_land.at[s],
            send_sem=out_ss.at[s], recv_sem=out_rs.at[s],
            device_id=(to_r, to_d), device_id_type=MESH,
        )

    def start_out(s, carry):
        out_copy(s).start()
        return carry

    lax.fori_loop(1, devices, start_out, 0)
    out_land[0] = out_send[me_r, me_d]

    mine = group == me_r
    wanted = fold(jnp.where(mine, target_v[...], 0.0))
    sigmas = fold(jnp.where(mine, sigma_v[...], 0.0))
    for s in range(1, domains):
        slot_copy(s).wait_recv()
    odd = lax.rem(me_d, per)
    rows = []
    for j in range(domains // per):
        total = None
        for i in range(per):
            tile = slot_land[j * per + i]
            moved = None
            for n in range(per):
                shift = ((i - n) * CAPACITY) % LANES
                option = pltpu.roll(tile, shift, axis=1) if shift else tile
                moved = option if moved is None else jnp.where(odd == n, option, moved)
            moved = jnp.where(lane // CAPACITY == i, moved, 0.0)
            total = moved if total is None else total + moved
        rows.append(total[0:1].astype(i32))
    picks = jnp.concatenate(
        [jnp.where(iota((owned, LANES), 0) + 1 == row, 1.0, 0.0).astype(bf16) for row in rows], axis=1
    )

    def wait_out(s, carry):
        out_copy(s).wait_recv()
        return carry

    lax.fori_loop(1, devices, wait_out, 0)
    spread = []
    for s in range(domains):
        total = out_land[s]
        for r in range(1, replicas):
            total = total + out_land[r * domains + s]
        for g in range(replicas):
            spread.append(jnp.where(group == g, total, 0.0))
    mean = fold(dot3(picks, jnp.concatenate(spread, axis=0))) / replicas
    misfit = mean - wanted
    adjoint = misfit / (sigmas * sigmas + 0.5 * misfit * misfit) / replicas
    adjoints = pieces_of(adjoint)
    for s in range(domains):
        value = None
        for piece in adjoints:
            one_part = lax.dot_general(
                picks[:, (s // per) * LANES : (s // per + 1) * LANES], piece,
                (((0,), (0,)), ((), ())), preferred_element_type=f32,
            )[(s % per) * CAPACITY : (s % per + 1) * CAPACITY]
            value = one_part if value is None else value + one_part
        packed = None
        for g in range(replicas):
            piece = jnp.where(group == g, value[g * slab : (g + 1) * slab], 0.0)
            packed = piece if packed is None else packed + piece
        back_send[s] = packed

    def back_copy(n):
        s = lax.rem(n, domains)
        to = lax.rem(me_r + n // domains, replicas), lax.rem(me_d + domains - s, domains)
        return pltpu.make_async_remote_copy(
            src_ref=back_send.at[s], dst_ref=back_land.at[n],
            send_sem=back_ss.at[n], recv_sem=back_rs.at[n],
            device_id=to, device_id_type=MESH,
        )

    def start_back(n, carry):
        back_copy(n).start()
        return carry

    lax.fori_loop(1, devices, start_back, 0)
    back_land[0] = back_send[0]
    packed = None
    for g in range(replicas):
        piece = jnp.where(group == g, mean[g * chunk : (g + 1) * chunk], 0.0)
        packed = piece if packed is None else packed + piece
    mean_send[...] = packed

    def mean_copy(n):
        return pltpu.make_async_remote_copy(
            src_ref=mean_send, dst_ref=mean_land.at[n],
            send_sem=mean_ss.at[n], recv_sem=mean_rs.at[n],
            device_id=(lax.rem(me_r + n, replicas), me_d), device_id_type=MESH,
        )

    for n in range(1, replicas):
        mean_copy(n).start()
    mean_land[0] = packed

    def wait_back(n, carry):
        back_copy(n).wait_recv()
        return carry

    lax.fori_loop(1, devices, wait_back, 0)
    source = [lax.rem(me_r + replicas - q, replicas) for q in range(replicas)]
    for s in range(domains):
        messages = [back_land[source[q] * domains + s] for q in range(replicas)]
        ret[lax.rem(me_d + s, domains)] = jnp.concatenate(
            [turned(messages, g) for g in range(replicas)], axis=0
        )
    adj_e[...] = dot3(perm_b[...], ret[...].reshape(slots, LANES))
    def finish(a):
        turn = lax.rem(a, 2)
        flat = [jnp.sum(jnp.transpose(sums[turn, c]), axis=0, keepdims=True) for c in range(4)]
        here = pl.ds(pl.multiple_of(a * LANES, LANES), LANES)
        for c in range(3):
            f_ref[c, :, here] = x_v[c, :, here] * flat[0] - flat[c + 1]

    def forces(a, carry):
        turn = lax.rem(a, 2)
        for k in range(listed):
            b = lst[k, a]
            scale = (energy_unit * norm) * cw_v[b] * adj_e[pl.ds(a * listed + k, 1), :]
            coefs[k * 4 : k * 4 + 4, :] = jnp.concatenate([scale, m_v[b] * scale], axis=0)
        for h in range(0, LANES, STRIP):
            acc = [[jnp.zeros((8, LANES), f32) for _ in range(STRIP // 8)] for _ in range(4)]
            for k in range(listed):
                rows = [
                    jnp.broadcast_to(coefs[k * 4 + c : k * 4 + c + 1, :], (8, LANES)) for c in range(4)
                ]
                for q in range(STRIP // 8):
                    g = g_v[a * listed + k, h + q * 8 : h + q * 8 + 8, :]
                    for c in range(4):
                        acc[c][q] = acc[c][q] + g * rows[c]
            for c in range(4):
                for q in range(STRIP // 8):
                    sums[turn, c, h + q * 8 : h + q * 8 + 8, :] = acc[c][q]
        finish(lax.rem(a + blocks - 1, blocks))
        return carry

    sums[(blocks - 1) % 2] = jnp.zeros((4, LANES, LANES), f32)
    lax.fori_loop(0, blocks, forces, 0)
    finish(blocks - 1)
    for n in range(1, replicas):
        mean_copy(n).wait_recv()
    messages = [mean_land[source[q]] for q in range(replicas)]
    for g in range(replicas):
        mean_ref[g * chunk : (g + 1) * chunk, :] = turned(messages, g)

    def sent(s, carry):
        out_copy(s).wait_send()
        back_copy(s).wait_send()
        return carry

    lax.fori_loop(1, devices, sent, 0)
    for s in range(1, domains):
        slot_copy(s).wait_send()
    for n in range(1, replicas):
        mean_copy(n).wait_send()


def hand_over(f_h, mean_h, f_out, mean_out, sems):
    copies = [
        pltpu.make_async_copy(f_h, f_out, sems.at[0]),
        pltpu.make_async_copy(mean_h, mean_out, sems.at[1]),
    ]
    for copy in copies:
        copy.start()
    for copy in copies:
        copy.wait()


def shards(
    coords, atom_var, atom_weight, atoms_live, block_list, owner_map,
    comp_means, comp_var, comp_weight, target, noise_sigma,
):
    replicas = lax.axis_size("rep")
    domains = lax.axis_size("dom")
    blocks, listed = block_list.shape
    comp_blocks = owner_map.shape[0]
    owned = target.shape[0] // LANES
    entries = blocks * listed
    slots = domains * CAPACITY
    devices = domains * replicas
    slab = CAPACITY // replicas
    per = LANES // CAPACITY
    x = coords.transpose(1, 0, 2)
    cm = comp_means.reshape(3, comp_blocks, LANES).transpose(1, 0, 2)
    cv = comp_var.reshape(comp_blocks, 1, LANES)
    cw = comp_weight.reshape(comp_blocks, 1, LANES)
    whole = pl.BlockSpec(memory_space=VMEM)
    far = pl.BlockSpec(memory_space=pltpu.HBM)
    dma = pltpu.SemaphoreType.DMA
    forces, mean = pl.pallas_call(
        functools.partial(step_kernel, replicas, domains, blocks, listed, owned),
        in_specs=[far] * 11,
        out_specs=[whole] * 2,
        out_shape=[
            jax.ShapeDtypeStruct(x.shape, f32),
            jax.ShapeDtypeStruct((owned, LANES), f32),
        ],
        scratch_shapes=[
            SMEM((blocks,), i32),
            SMEM((listed, blocks), i32),
            SMEM((comp_blocks,), i32),
            VMEM(x.shape, f32),
            VMEM((blocks, LANES), f32),
            VMEM((blocks, LANES), f32),
            VMEM(cm.shape, f32),
            VMEM(cv.shape, f32),
            VMEM(cw.shape, f32),
            VMEM((owned, LANES), f32),
            VMEM((owned, LANES), f32),
            VMEM((entries, LANES, LANES), f32),
            VMEM((2, LANES, ROWS), bf16),
            VMEM((2, LANES, LANES), f32),
            VMEM((2, listed // 2, 32, 2 * LANES), bf16),
            VMEM((entries, LANES), f32),
            VMEM((entries, LANES), i32),
            VMEM((entries, LANES), i32),
            VMEM((slots, entries), bf16),
            VMEM((entries, slots), bf16),
            VMEM((slots // LANES, 8, LANES), f32),
            VMEM((domains, 8, LANES), f32),
            VMEM((replicas, domains, slab, LANES), f32),
            VMEM((devices, slab, LANES), f32),
            VMEM((domains, slab, LANES), f32),
            VMEM((devices, slab, LANES), f32),
            VMEM((domains, CAPACITY, LANES), f32),
            VMEM((entries, LANES), f32),
            VMEM((owned // replicas, LANES), f32),
            VMEM((replicas, owned // replicas, LANES), f32),
            VMEM((2, 4, LANES, LANES), f32),
            VMEM((4 * listed, LANES), f32),
            dma((11,)),
            dma((domains,)),
            dma((domains,)),
            dma((devices,)),
            dma((devices,)),
            dma((devices,)),
            dma((devices,)),
            dma((replicas,)),
            dma((replicas,)),
        ],
        compiler_params=pltpu.CompilerParams(
            collective_id=0, has_side_effects=True, vmem_limit_bytes=60 << 20
        ),
        name="step",
    )(
        atoms_live, block_list.T, owner_map, x,
        atom_var.reshape(blocks, LANES), atom_weight.reshape(blocks, LANES),
        cm, cv, cw, target.reshape(owned, LANES), noise_sigma.reshape(owned, LANES),
    )
    forces, mean = pl.pallas_call(
        hand_over,
        in_specs=[far] * 2,
        out_specs=[far] * 2,
        out_shape=[
            jax.ShapeDtypeStruct(x.shape, f32),
            jax.ShapeDtypeStruct((owned, LANES), f32),
        ],
        scratch_shapes=[dma((2,))],
        name="hand_over",
    )(forces, mean)
    return (mean.reshape(-1), forces.transpose(1, 0, 2))


def solution(mesh):
    return jax.shard_map(
        shards,
        mesh=mesh,
        in_specs=(
            P("rep", None, "dom"),
            P("dom"),
            P("dom"),
            P("dom"),
            P("dom", None),
            P(),
            P(),
            P(),
            P(),
            P("dom"),
            P("dom"),
        ),
        out_specs=(P("dom"), P("rep", None, "dom")),
        check_vma=False,
    )
```

```python
import functools
import math

import jax
import jax.numpy as jnp
from jax import lax
from jax.experimental import pallas as pl
from jax.experimental.pallas import tpu as pltpu
from jax.sharding import PartitionSpec as P

CAPACITY = 64
LANES = 128
STRIP = 32
ROWS = 64

energy_unit = 2.494
norm = (2.0 * math.pi) ** -1.5
half_log2e = -0.5 / math.log(2.0)
dead = -1.0e4
VMEM = pltpu.VMEM
SMEM = pltpu.SMEM
MESH = pl.DeviceIdType.MESH
f32, i32, bf16 = jnp.float32, jnp.int32, jnp.bfloat16


def split(value):
    second = value - value.astype(bf16).astype(f32)
    third = second - second.astype(bf16).astype(f32)
    return value, second, third


def pieces_of(value):
    return [piece.astype(bf16) for piece in split(value)]


def dot3(picks, value):
    total = None
    for piece in pieces_of(value):
        part = jnp.dot(picks, piece, preferred_element_type=f32)
        total = part if total is None else total + part
    return total


def iota(shape, axis):
    return lax.broadcasted_iota(i32, shape, axis)


def step_kernel(
    replicas, domains, blocks, listed, owned, dense,
    live_h, lst_h, owner_h, x_h, av_h, aw_h, m_h, cv_h, cw_h, target_h, sigma_h,
    f_ref, mean_ref,
    live, lst, owner, x_v, av_v, aw_v, m_v, cv_v, cw_v, target_v, sigma_v,
    g_v, lhs_s, avt_s, rhs_s, part, place_s, perm_a, perm_b, slot_send, slot_land,
    out_send, out_land, back_send, back_land, ret, adj_e, mean_send, mean_land, sums, coefs, gt_v, left_s, dense_s, back_picks,
    loads, slot_ss, slot_rs, out_ss, out_rs, back_ss, back_rs, mean_ss, mean_rs,
):
    me_r = lax.axis_index("rep")
    me_d = lax.axis_index("dom")
    entries = blocks * listed
    slots = domains * CAPACITY
    width = LANES // replicas
    slab = CAPACITY // replicas
    per = LANES // CAPACITY
    devices = replicas * domains
    chunk = owned // replicas
    fetches = [
        pltpu.make_async_copy(src, dst, loads.at[i])
        for i, (src, dst) in enumerate(
            [(lst_h, lst), (owner_h, owner), (live_h, live), (x_h, x_v), (av_h, av_v), (aw_h, aw_v),
             (m_h, m_v), (cv_h, cv_v), (cw_h, cw_v), (target_h, target_v), (sigma_h, sigma_v)]
        )
    ]
    for fetch in fetches:
        fetch.start()
    barrier = pltpu.get_barrier_semaphore()

    def peer(s):
        return lax.rem(me_r + s // domains, replicas), lax.rem(me_d + lax.rem(s, domains), domains)

    def greet(s, carry):
        pl.semaphore_signal(barrier, inc=1, device_id=peer(s), device_id_type=MESH)
        return carry

    lax.fori_loop(1, devices, greet, 0)
    for fetch in fetches[:6]:
        fetch.wait()

    lane = iota((1, LANES), 1)
    group = lane // width
    one = jnp.ones((1, LANES), f32)
    zero = jnp.zeros((1, LANES), f32)

    def places(a, carry):
        for k in range(listed):
            place_s[pl.ds(a * listed + k, 1), :] = jnp.full((1, LANES), owner[lst[k, a]], i32)
        return carry

    lax.fori_loop(0, blocks, places, 0)
    dev = lax.div(place_s[...], owned)
    slot = place_s[...] - dev * owned + 1
    hot = jnp.where(dev == lane, 1.0, 0.0)
    before = jnp.where(iota((entries, entries), 1) < iota((entries, entries), 0), 1.0, 0.0).astype(bf16)
    rank = jnp.dot(before, hot.astype(bf16), preferred_element_type=f32)
    rank = jnp.sum(rank * hot, axis=1, keepdims=True)
    place = dev * CAPACITY + jnp.broadcast_to(rank, (entries, LANES)).astype(i32)
    for j in range(slots // LANES):
        perm_b[:, j * LANES : (j + 1) * LANES] = jnp.where(place == lane + j * LANES, 1.0, 0.0).astype(bf16)
    place_f = place.astype(f32)
    for j in range(entries // LANES):
        row = jnp.transpose(place_f[j * LANES : (j + 1) * LANES])[0:1].astype(i32)
        perm_a[:, j * LANES : (j + 1) * LANES] = jnp.where(
            iota((slots, LANES), 0) == row, 1.0, 0.0
        ).astype(bf16)
    slot_c = jnp.dot(perm_a[...], slot.astype(f32).astype(bf16), preferred_element_type=f32)
    for j in range(slots // LANES):
        slot_send[j] = jnp.transpose(slot_c[j * LANES : (j + 1) * LANES])[0:8]

    def slot_copy(s):
        to = lax.rem(me_d + s, domains)
        return pltpu.make_async_remote_copy(
            src_ref=slot_send.at[to // per], dst_ref=slot_land.at[s],
            send_sem=slot_ss.at[s], recv_sem=slot_rs.at[s],
            device_id=(me_r, to), device_id_type=MESH,
        )

    for fetch in fetches[6:]:
        fetch.wait()
    none = jnp.zeros((8, LANES), f32)

    def prepare(a, turn):
        x = jnp.concatenate(
            [x_v[c, :, pl.ds(pl.multiple_of(a * LANES, LANES), LANES)] for c in range(3)], axis=0
        )
        xx = jnp.sum(x * x, axis=0, keepdims=True)
        av = av_v[pl.ds(a, 1), :]
        lw = jnp.where(lane < live[a], jnp.log2(aw_v[pl.ds(a, 1), :]), dead)
        left = jnp.concatenate(
            [half_log2e * -2.0 * x, half_log2e * one, half_log2e * xx + av * lw, lw, zero, zero], axis=0
        )
        l0, l1, l2 = split(left)
        big = jnp.concatenate([l0, l0, l1, l1, l0, l2, none, none], axis=0)
        lhs_s[turn] = jnp.transpose(big.astype(bf16))
        avt_s[turn] = jnp.transpose(jnp.broadcast_to(av, (LANES, LANES)))
        for k in range(listed):
            b = lst[k, a]
            m = m_v[b]
            mm = jnp.sum(m * m, axis=0, keepdims=True)
            r0, r1, r2 = split(jnp.concatenate([m, mm, one, cv_v[b], zero, zero], axis=0))
            here = slice((k % 2) * LANES, (k % 2 + 1) * LANES)
            rhs_s[turn, k // 2, 0:16, here] = jnp.concatenate([r0, r1], axis=0).astype(bf16)
            rhs_s[turn, k // 2, 16:32, here] = jnp.concatenate([r2, r0], axis=0).astype(bf16)

    blank = jnp.zeros((16, 2 * LANES), bf16)

    def pair_block(a, turn):
        lhs = lhs_s[turn]
        for k in range(0, listed, 2):
            upper, lower = rhs_s[turn, k // 2, 0:16], rhs_s[turn, k // 2, 16:32]
            rhs = jnp.concatenate([upper, upper, lower, blank], axis=0)
            scaled = jnp.dot(lhs, rhs, preferred_element_type=f32)
            for i in range(2):
                e = a * listed + k + i
                b = lst[k + i, a]
                cv = jnp.broadcast_to(cv_v[b], (8, LANES))
                total = jnp.zeros((8, LANES), f32)
                for h in range(0, LANES, 8):
                    root = lax.rsqrt(avt_s[turn, h : h + 8, :] + cv)
                    inv = root * root
                    ov = (root * inv) * jnp.exp2(scaled[h : h + 8, i * LANES : (i + 1) * LANES] * inv)
                    total = total + ov
                    g_v[e, h : h + 8, :] = ov * inv
                part[pl.ds(e, 1), :] = jnp.sum(total, axis=0, keepdims=True) * (norm * cw_v[b])
        prepare(lax.rem(a + 1, blocks), 1 - turn)

    def pairs(n, carry):
        pair_block(2 * n, 0)
        pair_block(2 * n + 1, 1)
        return carry

    prepare(0, 0)
    early = blocks // 8
    lax.fori_loop(0, early, pairs, 0)
    pl.semaphore_wait(barrier, devices - 1)
    for s in range(1, domains):
        slot_copy(s).start()
    slot_land[0] = slot_send[me_d // per]
    lax.fori_loop(early, blocks // 2, pairs, 0)

    def turned(pieces, to):
        total = None
        for g in range(replicas):
            shift = (width * (g - to)) % LANES
            piece = pltpu.roll(pieces[g], shift, axis=1) if shift else pieces[g]
            piece = jnp.where(group == g, piece, 0.0)
            total = piece if total is None else total + piece
        return total

    def fold(value):
        shift = width
        while shift < LANES:
            value = value + pltpu.roll(value, shift, axis=1)
            shift = 2 * shift
        return value

    placed = dot3(perm_a[...], part[...]).reshape(domains, replicas, slab, LANES)
    parts = [placed[:, g].reshape(domains * slab, LANES) for g in range(replicas)]
    for q in range(replicas):
        out_send[q] = turned(parts, q).reshape(domains, slab, LANES)

    def out_copy(s):
        to_r, to_d = peer(s)
        return pltpu.make_async_remote_copy(
            src_ref=out_send.at[to_r, to_d], dst_ref=out_land.at[s],
            send_sem=out_ss.at[s], recv_sem=out_rs.at[s],
            device_id=(to_r, to_d), device_id_type=MESH,
        )

    def start_out(s, carry):
        out_copy(s).start()
        return carry

    lax.fori_loop(1, devices, start_out, 0)
    out_land[0] = out_send[me_r, me_d]

    def convert(a, carry):
        for k in range(dense):
            turned_g = jnp.transpose(g_v[a * listed + listed - dense + k])
            high = turned_g.astype(bf16)
            low = (turned_g - high.astype(f32)).astype(bf16)
            gt_v[a, k * LANES : (k + 1) * LANES, 0:LANES] = high
            gt_v[a, k * LANES : (k + 1) * LANES, LANES : 2 * LANES] = low
        return carry

    mine = group == me_r
    wanted = fold(jnp.where(mine, target_v[...], 0.0))
    sigmas = fold(jnp.where(mine, sigma_v[...], 0.0))
    for s in range(1, domains):
        slot_copy(s).wait_recv()
    odd = lax.rem(me_d, per)
    rows = []
    for j in range(domains // per):
        total = None
        for i in range(per):
            tile = slot_land[j * per + i]
            moved = None
            for n in range(per):
                shift = ((i - n) * CAPACITY) % LANES
                option = pltpu.roll(tile, shift, axis=1) if shift else tile
                moved = option if moved is None else jnp.where(odd == n, option, moved)
            moved = jnp.where(lane // CAPACITY == i, moved, 0.0)
            total = moved if total is None else total + moved
        rows.append(total[0:1])
    picks = jnp.concatenate(
        [jnp.where(iota((owned, LANES), 0) + 1 == row.astype(i32), 1.0, 0.0).astype(bf16) for row in rows],
        axis=1,
    )
    for j in range(domains // per):
        column = jnp.transpose(jnp.broadcast_to(rows[j], (LANES, LANES))).astype(i32)
        for i in range(max(1, owned // LANES)):
            span = min(owned, LANES)
            back_picks[j, :, i * span : (i + 1) * span] = jnp.where(
                column[:, :span] == iota((1, span), 1) + (i * span + 1), 1.0, 0.0
            ).astype(bf16)
    lax.fori_loop(0, blocks // 2, convert, 0)

    def wait_out(s, carry):
        out_copy(s).wait_recv()
        return carry

    lax.fori_loop(1, devices, wait_out, 0)
    spread = []
    for s in range(domains):
        total = out_land[s]
        for r in range(1, replicas):
            total = total + out_land[r * domains + s]
        for g in range(replicas):
            spread.append(jnp.where(group == g, total, 0.0))
    mean = fold(dot3(picks, jnp.concatenate(spread, axis=0))) / replicas
    misfit = mean - wanted
    adjoint = misfit / (sigmas * sigmas + 0.5 * misfit * misfit) / replicas
    adjoints = pieces_of(adjoint)
    for j in range(domains // per):
        value = None
        for piece in adjoints:
            part_j = jnp.dot(back_picks[j], piece, preferred_element_type=f32)
            value = part_j if value is None else value + part_j
        for i in range(per):
            packed = None
            for g in range(replicas):
                at = i * CAPACITY + g * slab
                piece = jnp.where(group == g, value[at : at + slab], 0.0)
                packed = piece if packed is None else packed + piece
            back_send[j * per + i] = packed

    def back_copy(n):
        s = lax.rem(n, domains)
        to = lax.rem(me_r + n // domains, replicas), lax.rem(me_d + domains - s, domains)
        return pltpu.make_async_remote_copy(
            src_ref=back_send.at[s], dst_ref=back_land.at[n],
            send_sem=back_ss.at[n], recv_sem=back_rs.at[n],
            device_id=to, device_id_type=MESH,
        )

    def start_back(n, carry):
        back_copy(n).start()
        return carry

    lax.fori_loop(1, devices, start_back, 0)
    back_land[0] = back_send[0]
    packed = None
    for g in range(replicas):
        piece = jnp.where(group == g, mean[g * chunk : (g + 1) * chunk], 0.0)
        packed = piece if packed is None else packed + piece
    mean_send[...] = packed

    def mean_copy(n):
        return pltpu.make_async_remote_copy(
            src_ref=mean_send, dst_ref=mean_land.at[n],
            send_sem=mean_ss.at[n], recv_sem=mean_rs.at[n],
            device_id=(lax.rem(me_r + n, replicas), me_d), device_id_type=MESH,
        )

    for n in range(1, replicas):
        mean_copy(n).start()
    mean_land[0] = packed

    lax.fori_loop(blocks // 2, blocks, convert, 0)

    def wait_back(n, carry):
        back_copy(n).wait_recv()
        return carry

    lax.fori_loop(1, devices, wait_back, 0)
    source = [lax.rem(me_r + replicas - q, replicas) for q in range(replicas)]
    for s in range(domains):
        messages = [back_land[source[q] * domains + s] for q in range(replicas)]
        ret[lax.rem(me_d + s, domains)] = jnp.concatenate(
            [turned(messages, g) for g in range(replicas)], axis=0
        )
    adj_e[...] = dot3(perm_b[...], ret[...].reshape(slots, LANES))
    def ready(a, turn):
        for k in range(listed):
            b = lst[k, a]
            scale = (energy_unit * norm) * cw_v[b] * adj_e[pl.ds(a * listed + k, 1), :]
            rows = jnp.concatenate([scale, m_v[b] * scale], axis=0)
            if k < listed - dense:
                coefs[turn, k * 4 : k * 4 + 4, :] = rows
            else:
                at = k - listed + dense
                stack = jnp.concatenate([*split(rows), jnp.zeros((4, LANES), f32)], axis=0)
                left_s[turn, :, at * LANES : (at + 1) * LANES] = stack.astype(bf16)

    def finish(a, turn):
        flat = [jnp.sum(jnp.transpose(sums[turn, c]), axis=0, keepdims=True) for c in range(4)]
        both = dense_s[turn, :, 0:LANES] + dense_s[turn, :, LANES : 2 * LANES]
        flat = [flat[c] + (both[c : c + 1] + both[c + 4 : c + 5] + both[c + 8 : c + 9]) for c in range(4)]
        here = pl.ds(pl.multiple_of(a * LANES, LANES), LANES)
        for c in range(3):
            f_ref[c, :, here] = x_v[c, :, here] * flat[0] - flat[c + 1]

    def force_block(a, turn):
        finish(lax.rem(a + blocks - 1, blocks), 1 - turn)
        dense_total = jnp.zeros((16, 2 * LANES), f32)
        for h in range(0, LANES, STRIP):
            share = dense * STRIP // LANES
            if share:
                here = slice(h // STRIP * share * LANES, (h // STRIP + 1) * share * LANES)
                dense_total = dense_total + jnp.dot(
                    left_s[turn, :, here], gt_v[a, here, :], preferred_element_type=f32
                )
            acc = [[jnp.zeros((8, LANES), f32) for _ in range(STRIP // 8)] for _ in range(4)]
            for k in range(listed - dense):
                rows = [
                    jnp.broadcast_to(coefs[turn, k * 4 + c : k * 4 + c + 1, :], (8, LANES)) for c in range(4)
                ]
                for q in range(STRIP // 8):
                    g = g_v[a * listed + k, h + q * 8 : h + q * 8 + 8, :]
                    for c in range(4):
                        acc[c][q] = acc[c][q] + g * rows[c]
            for c in range(4):
                for q in range(STRIP // 8):
                    sums[turn, c, h + q * 8 : h + q * 8 + 8, :] = acc[c][q]
        dense_s[turn] = dense_total
        ready(lax.rem(a + 1, blocks), 1 - turn)

    def forces(n, carry):
        force_block(2 * n, 0)
        force_block(2 * n + 1, 1)
        return carry

    ready(0, 0)
    sums[1] = jnp.zeros((4, LANES, LANES), f32)
    dense_s[1] = jnp.zeros((16, 2 * LANES), f32)
    lax.fori_loop(0, blocks // 2, forces, 0)
    finish(blocks - 1, 1)
    for n in range(1, replicas):
        mean_copy(n).wait_recv()
    messages = [mean_land[source[q]] for q in range(replicas)]
    for g in range(replicas):
        mean_ref[g * chunk : (g + 1) * chunk, :] = turned(messages, g)

    def sent(s, carry):
        out_copy(s).wait_send()
        back_copy(s).wait_send()
        return carry

    lax.fori_loop(1, devices, sent, 0)
    for s in range(1, domains):
        slot_copy(s).wait_send()
    for n in range(1, replicas):
        mean_copy(n).wait_send()


def hand_over(f_ref, mean_ref, f_out, mean_out):
    f_out[...] = f_ref[...]
    mean_out[...] = mean_ref[...]


def shards(
    coords, atom_var, atom_weight, atoms_live, block_list, owner_map,
    comp_means, comp_var, comp_weight, target, noise_sigma,
):
    replicas = lax.axis_size("rep")
    domains = lax.axis_size("dom")
    blocks, listed = block_list.shape
    comp_blocks = owner_map.shape[0]
    owned = target.shape[0] // LANES
    entries = blocks * listed
    slots = domains * CAPACITY
    devices = domains * replicas
    slab = CAPACITY // replicas
    per = LANES // CAPACITY
    dense = listed // 2 if slots == entries else listed // 4
    x = coords.transpose(1, 0, 2)
    cm = comp_means.reshape(3, comp_blocks, LANES).transpose(1, 0, 2)
    cv = comp_var.reshape(comp_blocks, 1, LANES)
    cw = comp_weight.reshape(comp_blocks, 1, LANES)
    whole = pl.BlockSpec(memory_space=VMEM)
    far = pl.BlockSpec(memory_space=pltpu.HBM)
    dma = pltpu.SemaphoreType.DMA
    forces, mean = pl.pallas_call(
        functools.partial(step_kernel, replicas, domains, blocks, listed, owned, dense),
        in_specs=[far] * 11,
        out_specs=[whole] * 2,
        out_shape=[
            jax.ShapeDtypeStruct(x.shape, f32),
            jax.ShapeDtypeStruct((owned, LANES), f32),
        ],
        scratch_shapes=[
            SMEM((blocks,), i32),
            SMEM((listed, blocks), i32),
            SMEM((comp_blocks,), i32),
            VMEM(x.shape, f32),
            VMEM((blocks, LANES), f32),
            VMEM((blocks, LANES), f32),
            VMEM(cm.shape, f32),
            VMEM(cv.shape, f32),
            VMEM(cw.shape, f32),
            VMEM((owned, LANES), f32),
            VMEM((owned, LANES), f32),
            VMEM((entries, LANES, LANES), f32),
            VMEM((2, LANES, ROWS), bf16),
            VMEM((2, LANES, LANES), f32),
            VMEM((2, listed // 2, 32, 2 * LANES), bf16),
            VMEM((entries, LANES), f32),
            VMEM((entries, LANES), i32),
            VMEM((slots, entries), bf16),
            VMEM((entries, slots), bf16),
            VMEM((slots // LANES, 8, LANES), f32),
            VMEM((domains, 8, LANES), f32),
            VMEM((replicas, domains, slab, LANES), f32),
            VMEM((devices, slab, LANES), f32),
            VMEM((domains, slab, LANES), f32),
            VMEM((devices, slab, LANES), f32),
            VMEM((domains, CAPACITY, LANES), f32),
            VMEM((entries, LANES), f32),
            VMEM((owned // replicas, LANES), f32),
            VMEM((replicas, owned // replicas, LANES), f32),
            VMEM((2, 4, LANES, LANES), f32),
            VMEM((2, 4 * (listed - dense), LANES), f32),
            VMEM((blocks, dense * LANES, 2 * LANES), bf16),
            VMEM((2, 16, dense * LANES), bf16),
            VMEM((2, 16, 2 * LANES), f32),
            VMEM((domains // per, LANES, owned), bf16),
            dma((11,)),
            dma((domains,)),
            dma((domains,)),
            dma((devices,)),
            dma((devices,)),
            dma((devices,)),
            dma((devices,)),
            dma((replicas,)),
            dma((replicas,)),
        ],
        compiler_params=pltpu.CompilerParams(
            collective_id=0, has_side_effects=True, vmem_limit_bytes=62 << 20
        ),
        name="step",
    )(
        atoms_live, block_list.T, owner_map, x,
        atom_var.reshape(blocks, LANES), atom_weight.reshape(blocks, LANES),
        cm, cv, cw, target.reshape(owned, LANES), noise_sigma.reshape(owned, LANES),
    )
    forces, mean = pl.pallas_call(
        hand_over,
        in_specs=[whole] * 2,
        out_specs=[whole] * 2,
        out_shape=[
            jax.ShapeDtypeStruct(x.shape, f32),
            jax.ShapeDtypeStruct((owned, LANES), f32),
        ],
        name="hand_over",
    )(forces, mean)
    return (mean.reshape(-1), forces.transpose(1, 0, 2))


def solution(mesh):
    return jax.shard_map(
        shards,
        mesh=mesh,
        in_specs=(
            P("rep", None, "dom"),
            P("dom"),
            P("dom"),
            P("dom"),
            P("dom", None),
            P(),
            P(),
            P(),
            P(),
            P("dom"),
            P("dom"),
        ),
        out_specs=(P("dom"), P("rep", None, "dom")),
        check_vma=False,
    )
```

```python
import functools
import math

import jax
import jax.numpy as jnp
from jax import lax
from jax.experimental import pallas as pl
from jax.experimental.pallas import tpu as pltpu
from jax.sharding import PartitionSpec as P

CAPACITY = 64
LANES = 128
STRIP = 32
ROWS = 64

energy_unit = 2.494
norm = (2.0 * math.pi) ** -1.5
half_log2e = -0.5 / math.log(2.0)
dead = -1.0e4
VMEM = pltpu.VMEM
SMEM = pltpu.SMEM
MESH = pl.DeviceIdType.MESH
f32, i32, bf16 = jnp.float32, jnp.int32, jnp.bfloat16


def split(value):
    second = value - value.astype(bf16).astype(f32)
    third = second - second.astype(bf16).astype(f32)
    return value, second, third


def pieces_of(value):
    return [piece.astype(bf16) for piece in split(value)]


def routed(picks, value):
    total = None
    for piece in pieces_of(value)[:2]:
        part = jnp.dot(picks, piece, preferred_element_type=f32)
        total = part if total is None else total + part
    return total


def iota(shape, axis):
    return lax.broadcasted_iota(i32, shape, axis)


def step_kernel(
    replicas, domains, blocks, listed, owned, dense,
    live_h, lst_h, owner_h, x_h, av_h, aw_h, m_h, cv_h, cw_h, target_h, sigma_h,
    f_ref, mean_ref,
    live, lst, owner, x_v, av_v, aw_v, table, target_v, sigma_v,
    g_v, lhs_s, avt_s, sum_s, cws, rhs_s, part, place_s, perm_a, perm_b, slot_send, slot_land,
    out_send, out_land, back_send, back_land, ret, adj_e, mean_send, mean_land, sums, coefs, gt_v, left_s, dense_s, back_picks,
    loads, slot_ss, slot_rs, out_ss, out_rs, back_ss, back_rs, mean_ss, mean_rs,
):
    me_r = lax.axis_index("rep")
    me_d = lax.axis_index("dom")
    entries = blocks * listed
    slots = domains * CAPACITY
    width = LANES // replicas
    slab = CAPACITY // replicas
    per = LANES // CAPACITY
    devices = replicas * domains
    chunk = owned // replicas
    fetches = [
        pltpu.make_async_copy(src, dst, loads.at[i])
        for i, (src, dst) in enumerate(
            [(lst_h, lst), (owner_h, owner), (live_h, live), (x_h, x_v), (av_h, av_v), (aw_h, aw_v),
             (m_h, table.at[:, 0:3, :]), (cv_h, table.at[:, 3:4, :]), (cw_h, table.at[:, 4:5, :]), (target_h, target_v), (sigma_h, sigma_v)]
        )
    ]
    for fetch in fetches:
        fetch.start()
    barrier = pltpu.get_barrier_semaphore()

    def peer(s):
        return lax.rem(me_r + s // domains, replicas), lax.rem(me_d + lax.rem(s, domains), domains)

    def greet(s, carry):
        pl.semaphore_signal(barrier, inc=1, device_id=peer(s), device_id_type=MESH)
        return carry

    lax.fori_loop(1, devices, greet, 0)
    for fetch in fetches[:6]:
        fetch.wait()

    lane = iota((1, LANES), 1)
    group = lane // width
    one = jnp.ones((1, LANES), f32)
    zero = jnp.zeros((1, LANES), f32)

    def places(a, carry):
        for k in range(listed):
            place_s[pl.ds(a * listed + k, 1), :] = jnp.full((1, LANES), owner[lst[k, a]], i32)
        return carry

    lax.fori_loop(0, blocks, places, 0)
    dev = lax.div(place_s[...], owned)
    slot = place_s[...] - dev * owned + 1
    hot = jnp.where(dev == lane, 1.0, 0.0)
    before = jnp.where(iota((entries, entries), 1) < iota((entries, entries), 0), 1.0, 0.0).astype(bf16)
    rank = jnp.dot(before, hot.astype(bf16), preferred_element_type=f32)
    rank = jnp.sum(rank * hot, axis=1, keepdims=True)
    place = dev * CAPACITY + jnp.broadcast_to(rank, (entries, LANES)).astype(i32)
    for j in range(slots // LANES):
        perm_b[:, j * LANES : (j + 1) * LANES] = jnp.where(place == lane + j * LANES, 1.0, 0.0).astype(bf16)
    place_f = place.astype(f32)
    for j in range(entries // LANES):
        row = jnp.transpose(place_f[j * LANES : (j + 1) * LANES])[0:1].astype(i32)
        perm_a[:, j * LANES : (j + 1) * LANES] = jnp.where(
            iota((slots, LANES), 0) == row, 1.0, 0.0
        ).astype(bf16)
    slot_c = jnp.dot(perm_a[...], slot.astype(f32).astype(bf16), preferred_element_type=f32)
    for j in range(slots // LANES):
        slot_send[j] = jnp.transpose(slot_c[j * LANES : (j + 1) * LANES])[0:8]

    def slot_copy(s):
        to = lax.rem(me_d + s, domains)
        return pltpu.make_async_remote_copy(
            src_ref=slot_send.at[to // per], dst_ref=slot_land.at[s],
            send_sem=slot_ss.at[s], recv_sem=slot_rs.at[s],
            device_id=(me_r, to), device_id_type=MESH,
        )

    for fetch in fetches[6:]:
        fetch.wait()
    none = jnp.zeros((8, LANES), f32)
    row8 = iota((8, LANES), 0)
    fourth = jnp.where(row8 == 3, 1.0, 0.0)

    def last(value):
        return jnp.where(row8 == 7, jnp.broadcast_to(value, (8, LANES)), 0.0)

    def prepare(a, turn):
        x = jnp.concatenate(
            [x_v[c, :, pl.ds(pl.multiple_of(a * LANES, LANES), LANES)] for c in range(3)], axis=0
        )
        xx = jnp.sum(x * x, axis=0, keepdims=True)
        av = av_v[pl.ds(a, 1), :]
        lw = jnp.where(lane < live[a], jnp.log2(aw_v[pl.ds(a, 1), :]), dead)
        half = half_log2e * one
        left = jnp.concatenate([half_log2e * -2.0 * x, lw, half, half, half, half * xx + av * lw], axis=0)
        l0, l1, l2 = split(left)
        a0, a1, a2 = split(av)
        scaled_rows = jnp.concatenate([l0, l0, l1, l1, l0, l2, none, none], axis=0)
        width_rows = jnp.concatenate(
            [fourth + last(a0), fourth, last(a1), none, fourth, last(a2), none, none], axis=0
        )
        lhs_s[turn, 0:LANES] = jnp.transpose(scaled_rows.astype(bf16))
        lhs_s[turn, LANES : 2 * LANES] = jnp.transpose(width_rows.astype(bf16))
        avt_s[turn] = jnp.transpose(jnp.broadcast_to(av, (LANES, LANES)))
        for k in range(listed):
            tile = table[lst[k, a]]
            squares = pltpu.roll(tile * tile, 4, axis=0)
            r0, r1, r2 = split(jnp.where(row8 < 4, tile, jnp.where(row8 == 7, 1.0, squares)))
            here = slice((k % 2) * LANES, (k % 2 + 1) * LANES)
            rhs_s[turn, k // 2, 0:16, here] = jnp.concatenate([r0, r1], axis=0).astype(bf16)
            rhs_s[turn, k // 2, 16:32, here] = jnp.concatenate([r2, r0], axis=0).astype(bf16)

    def gather(a, turn):
        for h in range(0, listed, 8):
            total = sum_s[turn, pl.ds(h * 8, 8, stride=8), :]
            for r in range(1, 8):
                total = total + sum_s[turn, pl.ds(h * 8 + r, 8, stride=8), :]
            part[pl.ds(pl.multiple_of(a * listed + h, 8), 8), :] = total * (norm * cws[turn, h : h + 8, :])

    blank = jnp.zeros((16, 2 * LANES), bf16)

    def pair_block(a, turn):
        gather(lax.rem(a + blocks - 1, blocks), 1 - turn)
        for k in range(0, listed, 2):
            upper, lower = rhs_s[turn, k // 2, 0:16], rhs_s[turn, k // 2, 16:32]
            rhs = jnp.concatenate([upper, upper, lower, blank], axis=0)
            both = k % 4 == 0
            lhs = lhs_s[turn] if both else lhs_s[turn, 0:LANES]
            scaled = jnp.dot(lhs, rhs, preferred_element_type=f32)
            for i in range(2):
                e = a * listed + k + i
                b = lst[k + i, a]
                if not both:
                    cv = jnp.broadcast_to(table[b, 3:4, :], (8, LANES))
                total = jnp.zeros((8, LANES), f32)
                here = slice(i * LANES, (i + 1) * LANES)
                for h in range(0, LANES, 8):
                    if both:
                        root = lax.rsqrt(scaled[LANES + h : LANES + h + 8, here])
                    else:
                        root = lax.rsqrt(avt_s[turn, h : h + 8, :] + cv)
                    inv = root * root
                    ov = (root * inv) * jnp.exp2(scaled[h : h + 8, here] * inv)
                    total = total + ov
                    g_v[e, h : h + 8, :] = ov * inv
                sum_s[turn, (k + i) * 8 : (k + i) * 8 + 8, :] = total
                cws[turn, k + i : k + i + 1, :] = table[b, 4:5, :]
        prepare(lax.rem(a + 1, blocks), 1 - turn)

    def pairs(n, carry):
        pair_block(2 * n, 0)
        pair_block(2 * n + 1, 1)
        return carry

    sum_s[1] = jnp.zeros((8 * listed, LANES), f32)
    cws[1] = jnp.zeros((listed, LANES), f32)
    prepare(0, 0)
    early = blocks // 8
    lax.fori_loop(0, early, pairs, 0)
    pl.semaphore_wait(barrier, devices - 1)
    for s in range(1, domains):
        slot_copy(s).start()
    slot_land[0] = slot_send[me_d // per]
    lax.fori_loop(early, blocks // 2, pairs, 0)
    gather(blocks - 1, 1)

    def turned(pieces, to):
        total = None
        for g in range(replicas):
            shift = (width * (g - to)) % LANES
            piece = pltpu.roll(pieces[g], shift, axis=1) if shift else pieces[g]
            piece = jnp.where(group == g, piece, 0.0)
            total = piece if total is None else total + piece
        return total

    def fold(value):
        shift = width
        while shift < LANES:
            value = value + pltpu.roll(value, shift, axis=1)
            shift = 2 * shift
        return value

    placed = routed(perm_a[...], part[...]).reshape(domains, replicas, slab, LANES)
    parts = [placed[:, g].reshape(domains * slab, LANES) for g in range(replicas)]
    for q in range(replicas):
        out_send[q] = turned(parts, q).reshape(domains, slab, LANES)

    def out_copy(s):
        to_r, to_d = peer(s)
        return pltpu.make_async_remote_copy(
            src_ref=out_send.at[to_r, to_d], dst_ref=out_land.at[s],
            send_sem=out_ss, recv_sem=out_rs,
            device_id=(to_r, to_d), device_id_type=MESH,
        )

    def all_of(land, send_sem, recv_sem):
        others = land.at[pl.ds(1, devices - 1)]
        return pltpu.make_async_remote_copy(
            src_ref=others, dst_ref=others, send_sem=send_sem, recv_sem=recv_sem,
            device_id=peer(1), device_id_type=MESH,
        )

    def start_out(s, carry):
        out_copy(s).start()
        return carry

    lax.fori_loop(1, devices, start_out, 0)
    out_land[0] = out_send[me_r, me_d]

    def convert(a, carry):
        for k in range(dense):
            turned_g = jnp.transpose(g_v[a * listed + listed - dense + k])
            high = turned_g.astype(bf16)
            low = (turned_g - high.astype(f32)).astype(bf16)
            gt_v[a, k * LANES : (k + 1) * LANES, 0:LANES] = high
            gt_v[a, k * LANES : (k + 1) * LANES, LANES : 2 * LANES] = low
        return carry

    mine = group == me_r
    wanted = fold(jnp.where(mine, target_v[...], 0.0))
    sigmas = fold(jnp.where(mine, sigma_v[...], 0.0))
    for s in range(1, domains):
        slot_copy(s).wait_recv()
    odd = lax.rem(me_d, per)
    rows = []
    for j in range(domains // per):
        total = None
        for i in range(per):
            tile = slot_land[j * per + i]
            moved = None
            for n in range(per):
                shift = ((i - n) * CAPACITY) % LANES
                option = pltpu.roll(tile, shift, axis=1) if shift else tile
                moved = option if moved is None else jnp.where(odd == n, option, moved)
            moved = jnp.where(lane // CAPACITY == i, moved, 0.0)
            total = moved if total is None else total + moved
        rows.append(total[0:1])
    picks = jnp.concatenate(
        [jnp.where(iota((owned, LANES), 0) + 1 == row.astype(i32), 1.0, 0.0).astype(bf16) for row in rows],
        axis=1,
    )
    for j in range(domains // per):
        column = jnp.transpose(jnp.broadcast_to(rows[j], (LANES, LANES))).astype(i32)
        for i in range(max(1, owned // LANES)):
            span = min(owned, LANES)
            back_picks[j, :, i * span : (i + 1) * span] = jnp.where(
                column[:, :span] == iota((1, span), 1) + (i * span + 1), 1.0, 0.0
            ).astype(bf16)
    lax.fori_loop(0, blocks // 2, convert, 0)

    all_of(out_land, out_ss, out_rs).wait_recv()
    spread = []
    for s in range(domains):
        total = out_land[s]
        for r in range(1, replicas):
            total = total + out_land[r * domains + s]
        for g in range(replicas):
            spread.append(jnp.where(group == g, total, 0.0))
    mean = fold(routed(picks, jnp.concatenate(spread, axis=0))) / replicas
    misfit = mean - wanted
    adjoint = misfit / (sigmas * sigmas + 0.5 * misfit * misfit) / replicas
    adjoints = pieces_of(adjoint)[:2]
    for j in range(domains // per):
        value = None
        for piece in adjoints:
            part_j = jnp.dot(back_picks[j], piece, preferred_element_type=f32)
            value = part_j if value is None else value + part_j
        for i in range(per):
            packed = None
            for g in range(replicas):
                at = i * CAPACITY + g * slab
                piece = jnp.where(group == g, value[at : at + slab], 0.0)
                packed = piece if packed is None else packed + piece
            back_send[j * per + i] = packed

    def back_copy(n):
        s = lax.rem(n, domains)
        to = lax.rem(me_r + n // domains, replicas), lax.rem(me_d + domains - s, domains)
        return pltpu.make_async_remote_copy(
            src_ref=back_send.at[s], dst_ref=back_land.at[n],
            send_sem=back_ss, recv_sem=back_rs,
            device_id=to, device_id_type=MESH,
        )

    def start_back(n, carry):
        back_copy(n).start()
        return carry

    lax.fori_loop(1, devices, start_back, 0)
    back_land[0] = back_send[0]
    packed = None
    for g in range(replicas):
        piece = jnp.where(group == g, mean[g * chunk : (g + 1) * chunk], 0.0)
        packed = piece if packed is None else packed + piece
    mean_send[...] = packed

    def mean_copy(n):
        return pltpu.make_async_remote_copy(
            src_ref=mean_send, dst_ref=mean_land.at[n],
            send_sem=mean_ss.at[n], recv_sem=mean_rs.at[n],
            device_id=(lax.rem(me_r + n, replicas), me_d), device_id_type=MESH,
        )

    for n in range(1, replicas):
        mean_copy(n).start()
    mean_land[0] = packed

    lax.fori_loop(blocks // 2, blocks, convert, 0)

    all_of(back_land, back_ss, back_rs).wait_recv()
    source = [lax.rem(me_r + replicas - q, replicas) for q in range(replicas)]
    for s in range(domains):
        messages = [back_land[source[q] * domains + s] for q in range(replicas)]
        ret[lax.rem(me_d + s, domains)] = jnp.concatenate(
            [turned(messages, g) for g in range(replicas)], axis=0
        )
    adj_e[...] = routed(perm_b[...], ret[...].reshape(slots, LANES))
    def ready(a, turn):
        for k in range(listed):
            tile = table[lst[k, a]]
            scale = (energy_unit * norm) * tile[4:5] * adj_e[pl.ds(a * listed + k, 1), :]
            rows = (jnp.where(row8 == 3, 1.0, tile) * jnp.broadcast_to(scale, (8, LANES)))[0:4]
            if k < listed - dense:
                coefs[turn, k * 4 : k * 4 + 4, :] = rows
            else:
                at = k - listed + dense
                stack = jnp.concatenate([*split(rows), jnp.zeros((4, LANES), f32)], axis=0)
                left_s[turn, :, at * LANES : (at + 1) * LANES] = stack.astype(bf16)

    def finish(a, turn):
        flat = [jnp.sum(jnp.transpose(sums[turn, c]), axis=0, keepdims=True) for c in range(4)]
        both = dense_s[turn, :, 0:LANES] + dense_s[turn, :, LANES : 2 * LANES]
        flat = [flat[c] + (both[c : c + 1] + both[c + 4 : c + 5] + both[c + 8 : c + 9]) for c in range(4)]
        here = pl.ds(pl.multiple_of(a * LANES, LANES), LANES)
        for c in range(3):
            f_ref[c, :, here] = x_v[c, :, here] * flat[3] - flat[c]

    def force_block(a, turn):
        finish(lax.rem(a + blocks - 1, blocks), 1 - turn)
        dense_total = jnp.zeros((16, 2 * LANES), f32)
        for h in range(0, LANES, STRIP):
            share = dense * STRIP // LANES
            if share:
                here = slice(h // STRIP * share * LANES, (h // STRIP + 1) * share * LANES)
                dense_total = dense_total + jnp.dot(
                    left_s[turn, :, here], gt_v[a, here, :], preferred_element_type=f32
                )
            acc = [[jnp.zeros((8, LANES), f32) for _ in range(STRIP // 8)] for _ in range(4)]
            for k in range(listed - dense):
                rows = [
                    jnp.broadcast_to(coefs[turn, k * 4 + c : k * 4 + c + 1, :], (8, LANES)) for c in range(4)
                ]
                for q in range(STRIP // 8):
                    g = g_v[a * listed + k, h + q * 8 : h + q * 8 + 8, :]
                    for c in range(4):
                        acc[c][q] = acc[c][q] + g * rows[c]
            for c in range(4):
                for q in range(STRIP // 8):
                    sums[turn, c, h + q * 8 : h + q * 8 + 8, :] = acc[c][q]
        dense_s[turn] = dense_total
        ready(lax.rem(a + 1, blocks), 1 - turn)

    def forces(n, carry):
        force_block(2 * n, 0)
        force_block(2 * n + 1, 1)
        return carry

    ready(0, 0)
    sums[1] = jnp.zeros((4, LANES, LANES), f32)
    dense_s[1] = jnp.zeros((16, 2 * LANES), f32)
    lax.fori_loop(0, blocks // 2, forces, 0)
    finish(blocks - 1, 1)
    for n in range(1, replicas):
        mean_copy(n).wait_recv()
    messages = [mean_land[source[q]] for q in range(replicas)]
    for g in range(replicas):
        mean_ref[g * chunk : (g + 1) * chunk, :] = turned(messages, g)

    all_of(out_land, out_ss, out_rs).wait_send()
    all_of(back_land, back_ss, back_rs).wait_send()
    for s in range(1, domains):
        slot_copy(s).wait_send()
    for n in range(1, replicas):
        mean_copy(n).wait_send()


def hand_over(f_ref, mean_ref, f_out, mean_out):
    f_out[...] = f_ref[...]
    mean_out[...] = mean_ref[...]


def shards(
    coords, atom_var, atom_weight, atoms_live, block_list, owner_map,
    comp_means, comp_var, comp_weight, target, noise_sigma,
):
    replicas = lax.axis_size("rep")
    domains = lax.axis_size("dom")
    blocks, listed = block_list.shape
    comp_blocks = owner_map.shape[0]
    owned = target.shape[0] // LANES
    entries = blocks * listed
    slots = domains * CAPACITY
    devices = domains * replicas
    slab = CAPACITY // replicas
    per = LANES // CAPACITY
    dense = listed // 2 if slots == entries else listed // 4
    x = coords.transpose(1, 0, 2)
    cm = comp_means.reshape(3, comp_blocks, LANES).transpose(1, 0, 2)
    cv = comp_var.reshape(comp_blocks, 1, LANES)
    cw = comp_weight.reshape(comp_blocks, 1, LANES)
    whole = pl.BlockSpec(memory_space=VMEM)
    far = pl.BlockSpec(memory_space=pltpu.HBM)
    dma = pltpu.SemaphoreType.DMA
    forces, mean = pl.pallas_call(
        functools.partial(step_kernel, replicas, domains, blocks, listed, owned, dense),
        in_specs=[far] * 11,
        out_specs=[whole] * 2,
        out_shape=[
            jax.ShapeDtypeStruct(x.shape, f32),
            jax.ShapeDtypeStruct((owned, LANES), f32),
        ],
        scratch_shapes=[
            SMEM((blocks,), i32),
            SMEM((listed, blocks), i32),
            SMEM((comp_blocks,), i32),
            VMEM(x.shape, f32),
            VMEM((blocks, LANES), f32),
            VMEM((blocks, LANES), f32),
            VMEM((comp_blocks, 8, LANES), f32),
            VMEM((owned, LANES), f32),
            VMEM((owned, LANES), f32),
            VMEM((entries, LANES, LANES), f32),
            VMEM((2, 2 * LANES, ROWS), bf16),
            VMEM((2, LANES, LANES), f32),
            VMEM((2, 8 * listed, LANES), f32),
            VMEM((2, listed, LANES), f32),
            VMEM((2, listed // 2, 32, 2 * LANES), bf16),
            VMEM((entries, LANES), f32),
            VMEM((entries, LANES), i32),
            VMEM((slots, entries), bf16),
            VMEM((entries, slots), bf16),
            VMEM((slots // LANES, 8, LANES), f32),
            VMEM((domains, 8, LANES), f32),
            VMEM((replicas, domains, slab, LANES), f32),
            VMEM((devices, slab, LANES), f32),
            VMEM((domains, slab, LANES), f32),
            VMEM((devices, slab, LANES), f32),
            VMEM((domains, CAPACITY, LANES), f32),
            VMEM((entries, LANES), f32),
            VMEM((owned // replicas, LANES), f32),
            VMEM((replicas, owned // replicas, LANES), f32),
            VMEM((2, 4, LANES, LANES), f32),
            VMEM((2, 4 * (listed - dense), LANES), f32),
            VMEM((blocks, dense * LANES, 2 * LANES), bf16),
            VMEM((2, 16, dense * LANES), bf16),
            VMEM((2, 16, 2 * LANES), f32),
            VMEM((domains // per, LANES, owned), bf16),
            dma((11,)),
            dma((domains,)),
            dma((domains,)),
            dma,
            dma,
            dma,
            dma,
            dma((replicas,)),
            dma((replicas,)),
        ],
        compiler_params=pltpu.CompilerParams(
            collective_id=0, has_side_effects=True, vmem_limit_bytes=63 << 20
        ),
        name="step",
    )(
        atoms_live, block_list.T, owner_map, x,
        atom_var.reshape(blocks, LANES), atom_weight.reshape(blocks, LANES),
        cm, cv, cw, target.reshape(owned, LANES), noise_sigma.reshape(owned, LANES),
    )
    forces, mean = pl.pallas_call(
        hand_over,
        in_specs=[whole] * 2,
        out_specs=[whole] * 2,
        out_shape=[
            jax.ShapeDtypeStruct(x.shape, f32),
            jax.ShapeDtypeStruct((owned, LANES), f32),
        ],
        name="hand_over",
    )(forces, mean)
    return (mean.reshape(-1), forces.transpose(1, 0, 2))


def solution(mesh):
    return jax.shard_map(
        shards,
        mesh=mesh,
        in_specs=(
            P("rep", None, "dom"),
            P("dom"),
            P("dom"),
            P("dom"),
            P("dom", None),
            P(),
            P(),
            P(),
            P(),
            P("dom"),
            P("dom"),
        ),
        out_specs=(P("dom"), P("rep", None, "dom")),
        check_vma=False,
    )
```

```python
import functools
import math

import jax
import jax.numpy as jnp
from jax import lax
from jax.experimental import pallas as pl
from jax.experimental.pallas import tpu as pltpu
from jax.sharding import PartitionSpec as P

CAPACITY = 64
LANES = 128
STRIP = 32
ROWS = 64

energy_unit = 2.494
norm = (2.0 * math.pi) ** -1.5
half_log2e = -0.5 / math.log(2.0)
dead = -1.0e4
VMEM = pltpu.VMEM
SMEM = pltpu.SMEM
MESH = pl.DeviceIdType.MESH
f32, i32, bf16 = jnp.float32, jnp.int32, jnp.bfloat16


def split(value):
    second = value - value.astype(bf16).astype(f32)
    third = second - second.astype(bf16).astype(f32)
    return value, second, third


def pieces_of(value):
    return [piece.astype(bf16) for piece in split(value)]


def routed(picks, value):
    total = None
    for piece in pieces_of(value)[:2]:
        part = jnp.dot(picks, piece, preferred_element_type=f32)
        total = part if total is None else total + part
    return total


def iota(shape, axis):
    return lax.broadcasted_iota(i32, shape, axis)


def step_kernel(
    replicas, domains, blocks, listed, owned, dense,
    live_h, lst_h, owner_h, x_h, av_h, aw_h, m_h, cv_h, cw_h, target_h, sigma_h,
    f_ref, mean_ref,
    live, lst, owner, x_v, av_v, aw_v, table, target_v, sigma_v,
    g_v, lhs_s, avt_s, sum_s, cws, rhs_s, part, place_s, perm_a, perm_b, slot_send, slot_land,
    out_send, core_land, pair_send, out_land, back_send, back_land, ret, adj_e, mean_send, mean_land, sums, coefs, gt_v, left_s, dense_s, back_picks,
    loads, slot_ss, slot_rs, core_ss, core_rs, out_ss, out_rs, back_ss, back_rs, swap_ss, swap_rs, mean_ss, mean_rs,
):
    me_r = lax.axis_index("rep")
    me_d = lax.axis_index("dom")
    entries = blocks * listed
    slots = domains * CAPACITY
    width = LANES // replicas
    slab = CAPACITY // replicas
    per = LANES // CAPACITY
    devices = replicas * domains
    chunk = owned // replicas
    chips = replicas // 2
    cells = chips * domains
    core = lax.rem(me_r, 2)
    fetches = [
        pltpu.make_async_copy(src, dst, loads.at[i])
        for i, (src, dst) in enumerate(
            [(lst_h, lst), (owner_h, owner), (live_h, live), (x_h, x_v), (av_h, av_v), (aw_h, aw_v),
             (m_h, table.at[:, 0:3, :]), (cv_h, table.at[:, 3:4, :]), (cw_h, table.at[:, 4:5, :]), (target_h, target_v), (sigma_h, sigma_v)]
        )
    ]
    for fetch in fetches:
        fetch.start()
    barrier = pltpu.get_barrier_semaphore()

    def peer(s):
        return lax.rem(me_r + s // domains, replicas), lax.rem(me_d + lax.rem(s, domains), domains)

    def greet(s, carry):
        pl.semaphore_signal(barrier, inc=1, device_id=peer(s), device_id_type=MESH)
        return carry

    lax.fori_loop(1, devices, greet, 0)
    for fetch in fetches[:6]:
        fetch.wait()

    lane = iota((1, LANES), 1)
    group = lane // width
    one = jnp.ones((1, LANES), f32)
    zero = jnp.zeros((1, LANES), f32)

    def places(a, carry):
        for k in range(listed):
            place_s[pl.ds(a * listed + k, 1), :] = jnp.full((1, LANES), owner[lst[k, a]], i32)
        return carry

    lax.fori_loop(0, blocks, places, 0)
    dev = lax.div(place_s[...], owned)
    slot = place_s[...] - dev * owned + 1
    hot = jnp.where(dev == lane, 1.0, 0.0)
    before = jnp.where(iota((entries, entries), 1) < iota((entries, entries), 0), 1.0, 0.0).astype(bf16)
    rank = jnp.dot(before, hot.astype(bf16), preferred_element_type=f32)
    rank = jnp.sum(rank * hot, axis=1, keepdims=True)
    place = dev * CAPACITY + jnp.broadcast_to(rank, (entries, LANES)).astype(i32)
    for j in range(slots // LANES):
        perm_b[:, j * LANES : (j + 1) * LANES] = jnp.where(place == lane + j * LANES, 1.0, 0.0).astype(bf16)
    place_f = place.astype(f32)
    for j in range(entries // LANES):
        row = jnp.transpose(place_f[j * LANES : (j + 1) * LANES])[0:1].astype(i32)
        perm_a[:, j * LANES : (j + 1) * LANES] = jnp.where(
            iota((slots, LANES), 0) == row, 1.0, 0.0
        ).astype(bf16)
    slot_c = jnp.dot(perm_a[...], slot.astype(f32).astype(bf16), preferred_element_type=f32)
    for j in range(slots // LANES):
        slot_send[j] = jnp.transpose(slot_c[j * LANES : (j + 1) * LANES])[0:8]

    def slot_copy(s):
        to = lax.rem(me_d + s, domains)
        return pltpu.make_async_remote_copy(
            src_ref=slot_send.at[to // per], dst_ref=slot_land.at[s],
            send_sem=slot_ss.at[s], recv_sem=slot_rs.at[s],
            device_id=(me_r, to), device_id_type=MESH,
        )

    for fetch in fetches[6:]:
        fetch.wait()
    none = jnp.zeros((8, LANES), f32)
    row8 = iota((8, LANES), 0)
    fourth = jnp.where(row8 == 3, 1.0, 0.0)

    def last(value):
        return jnp.where(row8 == 7, jnp.broadcast_to(value, (8, LANES)), 0.0)

    def prepare(a, turn):
        x = jnp.concatenate(
            [x_v[c, :, pl.ds(pl.multiple_of(a * LANES, LANES), LANES)] for c in range(3)], axis=0
        )
        xx = jnp.sum(x * x, axis=0, keepdims=True)
        av = av_v[pl.ds(a, 1), :]
        lw = jnp.where(lane < live[a], jnp.log2(aw_v[pl.ds(a, 1), :]), dead)
        half = half_log2e * one
        left = jnp.concatenate([half_log2e * -2.0 * x, lw, half, half, half, half * xx + av * lw], axis=0)
        l0, l1, l2 = split(left)
        a0, a1, a2 = split(av)
        scaled_rows = jnp.concatenate([l0, l0, l1, l1, l0, l2, none, none], axis=0)
        width_rows = jnp.concatenate(
            [fourth + last(a0), fourth, last(a1), none, fourth, last(a2), none, none], axis=0
        )
        lhs_s[turn, 0:LANES] = jnp.transpose(scaled_rows.astype(bf16))
        lhs_s[turn, LANES : 2 * LANES] = jnp.transpose(width_rows.astype(bf16))
        avt_s[turn] = jnp.transpose(jnp.broadcast_to(av, (LANES, LANES)))
        for k in range(listed):
            tile = table[lst[k, a]]
            squares = pltpu.roll(tile * tile, 4, axis=0)
            r0, r1, r2 = split(jnp.where(row8 < 4, tile, jnp.where(row8 == 7, 1.0, squares)))
            here = slice((k % 2) * LANES, (k % 2 + 1) * LANES)
            rhs_s[turn, k // 2, 0:16, here] = jnp.concatenate([r0, r1], axis=0).astype(bf16)
            rhs_s[turn, k // 2, 16:32, here] = jnp.concatenate([r2, r0], axis=0).astype(bf16)

    def gather(a, turn):
        for h in range(0, listed, 8):
            total = sum_s[turn, pl.ds(h * 8, 8, stride=8), :]
            for r in range(1, 8):
                total = total + sum_s[turn, pl.ds(h * 8 + r, 8, stride=8), :]
            part[pl.ds(pl.multiple_of(a * listed + h, 8), 8), :] = total * (norm * cws[turn, h : h + 8, :])

    blank = jnp.zeros((16, 2 * LANES), bf16)

    def pair_block(a, turn):
        gather(lax.rem(a + blocks - 1, blocks), 1 - turn)
        for k in range(0, listed, 2):
            upper, lower = rhs_s[turn, k // 2, 0:16], rhs_s[turn, k // 2, 16:32]
            rhs = jnp.concatenate([upper, upper, lower, blank], axis=0)
            both = k % 4 == 0
            lhs = lhs_s[turn] if both else lhs_s[turn, 0:LANES]
            scaled = jnp.dot(lhs, rhs, preferred_element_type=f32)
            for i in range(2):
                e = a * listed + k + i
                b = lst[k + i, a]
                if not both:
                    cv = jnp.broadcast_to(table[b, 3:4, :], (8, LANES))
                total = jnp.zeros((8, LANES), f32)
                here = slice(i * LANES, (i + 1) * LANES)
                for h in range(0, LANES, 8):
                    if both:
                        root = lax.rsqrt(scaled[LANES + h : LANES + h + 8, here])
                    else:
                        root = lax.rsqrt(avt_s[turn, h : h + 8, :] + cv)
                    inv = root * root
                    ov = (root * inv) * jnp.exp2(scaled[h : h + 8, here] * inv)
                    total = total + ov
                    g_v[e, h : h + 8, :] = ov * inv
                sum_s[turn, (k + i) * 8 : (k + i) * 8 + 8, :] = total
                cws[turn, k + i : k + i + 1, :] = table[b, 4:5, :]
        prepare(lax.rem(a + 1, blocks), 1 - turn)

    def pairs(n, carry):
        pair_block(2 * n, 0)
        pair_block(2 * n + 1, 1)
        return carry

    sum_s[1] = jnp.zeros((8 * listed, LANES), f32)
    cws[1] = jnp.zeros((listed, LANES), f32)
    prepare(0, 0)
    early = blocks // 8
    lax.fori_loop(0, early, pairs, 0)
    pl.semaphore_wait(barrier, devices - 1)
    for s in range(1, domains):
        slot_copy(s).start()
    slot_land[0] = slot_send[me_d // per]
    lax.fori_loop(early, blocks // 2, pairs, 0)
    gather(blocks - 1, 1)

    def turned(pieces, to):
        total = None
        for g in range(replicas):
            shift = (width * (g - to)) % LANES
            piece = pltpu.roll(pieces[g], shift, axis=1) if shift else pieces[g]
            piece = jnp.where(group == g, piece, 0.0)
            total = piece if total is None else total + piece
        return total

    def fold(value):
        shift = width
        while shift < LANES:
            value = value + pltpu.roll(value, shift, axis=1)
            shift = 2 * shift
        return value

    placed = routed(perm_a[...], part[...]).reshape(domains, replicas, slab, LANES)
    parts = [placed[:, g].reshape(domains * slab, LANES) for g in range(replicas)]
    for q in range(replicas):
        out_send[q] = turned(parts, q).reshape(domains, slab, LANES)

    partner = (me_r + 1 - 2 * core, me_d)

    def core_copy(n):
        return pltpu.make_async_remote_copy(
            src_ref=out_send.at[2 * n + 1 - core], dst_ref=core_land.at[n],
            send_sem=core_ss.at[n], recv_sem=core_rs.at[n],
            device_id=partner, device_id_type=MESH,
        )

    def pair_peer(n, sign):
        to_r = lax.rem(me_r + 2 * (n // domains), replicas)
        return to_r, lax.rem(me_d + domains + sign * lax.rem(n, domains), domains)

    def out_copy(n):
        to_r, to_d = pair_peer(n, 1)
        return pltpu.make_async_remote_copy(
            src_ref=pair_send.at[to_r // 2, to_d], dst_ref=out_land.at[n],
            send_sem=out_ss, recv_sem=out_rs,
            device_id=(to_r, to_d), device_id_type=MESH,
        )

    def all_of(land, send_sem, recv_sem):
        others = land.at[pl.ds(1, cells - 1)]
        return pltpu.make_async_remote_copy(
            src_ref=others, dst_ref=others, send_sem=send_sem, recv_sem=recv_sem,
            device_id=partner, device_id_type=MESH,
        )

    def start_out(n, carry):
        out_copy(n).start()
        return carry

    for n in range(chips):
        core_copy(n).start()
    for n in range(chips):
        core_copy(n).wait_recv()
        pair_send[n] = out_send[2 * n + core] + core_land[n]
    lax.fori_loop(1, cells, start_out, 0)
    out_land[0] = pair_send[me_r // 2, me_d]

    def convert(a, carry):
        for k in range(dense):
            turned_g = jnp.transpose(g_v[a * listed + listed - dense + k])
            high = turned_g.astype(bf16)
            low = (turned_g - high.astype(f32)).astype(bf16)
            gt_v[a, k * LANES : (k + 1) * LANES, 0:LANES] = high
            gt_v[a, k * LANES : (k + 1) * LANES, LANES : 2 * LANES] = low
        return carry

    mine = group == me_r
    wanted = fold(jnp.where(mine, target_v[...], 0.0))
    sigmas = fold(jnp.where(mine, sigma_v[...], 0.0))
    for s in range(1, domains):
        slot_copy(s).wait_recv()
    odd = lax.rem(me_d, per)
    rows = []
    for j in range(domains // per):
        total = None
        for i in range(per):
            tile = slot_land[j * per + i]
            moved = None
            for n in range(per):
                shift = ((i - n) * CAPACITY) % LANES
                option = pltpu.roll(tile, shift, axis=1) if shift else tile
                moved = option if moved is None else jnp.where(odd == n, option, moved)
            moved = jnp.where(lane // CAPACITY == i, moved, 0.0)
            total = moved if total is None else total + moved
        rows.append(total[0:1])
    picks = jnp.concatenate(
        [jnp.where(iota((owned, LANES), 0) + 1 == row.astype(i32), 1.0, 0.0).astype(bf16) for row in rows],
        axis=1,
    )
    for j in range(domains // per):
        column = jnp.transpose(jnp.broadcast_to(rows[j], (LANES, LANES))).astype(i32)
        for i in range(max(1, owned // LANES)):
            span = min(owned, LANES)
            back_picks[j, :, i * span : (i + 1) * span] = jnp.where(
                column[:, :span] == iota((1, span), 1) + (i * span + 1), 1.0, 0.0
            ).astype(bf16)
    lax.fori_loop(0, blocks // 2, convert, 0)

    all_of(out_land, out_ss, out_rs).wait_recv()
    spread = []
    for s in range(domains):
        total = out_land[s]
        for r in range(1, chips):
            total = total + out_land[r * domains + s]
        for g in range(replicas):
            spread.append(jnp.where(group == g, total, 0.0))
    mean = fold(routed(picks, jnp.concatenate(spread, axis=0))) / replicas
    misfit = mean - wanted
    adjoint = misfit / (sigmas * sigmas + 0.5 * misfit * misfit) / replicas
    adjoints = pieces_of(adjoint)[:2]
    for j in range(domains // per):
        value = None
        for piece in adjoints:
            part_j = jnp.dot(back_picks[j], piece, preferred_element_type=f32)
            value = part_j if value is None else value + part_j
        for i in range(per):
            packed = None
            for g in range(replicas):
                at = i * CAPACITY + g * slab
                piece = jnp.where(group == g, value[at : at + slab], 0.0)
                packed = piece if packed is None else packed + piece
            back_send[j * per + i] = packed

    def back_copy(n):
        return pltpu.make_async_remote_copy(
            src_ref=back_send.at[lax.rem(n, domains)], dst_ref=back_land.at[0, n],
            send_sem=back_ss, recv_sem=back_rs,
            device_id=pair_peer(n, -1), device_id_type=MESH,
        )

    def start_back(n, carry):
        back_copy(n).start()
        return carry

    lax.fori_loop(1, cells, start_back, 0)
    back_land[0, 0] = back_send[0]
    packed = None
    for g in range(replicas):
        piece = jnp.where(group == g, mean[g * chunk : (g + 1) * chunk], 0.0)
        packed = piece if packed is None else packed + piece
    mean_send[...] = packed

    def mean_copy(n):
        return pltpu.make_async_remote_copy(
            src_ref=mean_send, dst_ref=mean_land.at[n],
            send_sem=mean_ss.at[n], recv_sem=mean_rs.at[n],
            device_id=(lax.rem(me_r + n, replicas), me_d), device_id_type=MESH,
        )

    for n in range(1, replicas):
        mean_copy(n).start()
    mean_land[0] = packed

    lax.fori_loop(blocks // 2, blocks, convert, 0)

    all_of(back_land.at[0], back_ss, back_rs).wait_recv()
    swap = pltpu.make_async_remote_copy(
        src_ref=back_land.at[0], dst_ref=back_land.at[1], send_sem=swap_ss, recv_sem=swap_rs,
        device_id=partner, device_id_type=MESH,
    )
    swap.start()
    swap.wait_recv()
    source = [lax.rem(me_r + replicas - q, replicas) for q in range(replicas)]
    for s in range(domains):
        messages = [
            back_land[lax.rem(core + q, 2), lax.rem(me_r // 2 + chips - q // 2, chips) * domains + s]
            for q in range(replicas)
        ]
        ret[lax.rem(me_d + s, domains)] = jnp.concatenate(
            [turned(messages, g) for g in range(replicas)], axis=0
        )
    adj_e[...] = routed(perm_b[...], ret[...].reshape(slots, LANES))
    def ready(a, turn):
        for k in range(listed):
            tile = table[lst[k, a]]
            scale = (energy_unit * norm) * tile[4:5] * adj_e[pl.ds(a * listed + k, 1), :]
            rows = (jnp.where(row8 == 3, 1.0, tile) * jnp.broadcast_to(scale, (8, LANES)))[0:4]
            if k < listed - dense:
                coefs[turn, k * 4 : k * 4 + 4, :] = rows
            else:
                at = k - listed + dense
                stack = jnp.concatenate([*split(rows), jnp.zeros((4, LANES), f32)], axis=0)
                left_s[turn, :, at * LANES : (at + 1) * LANES] = stack.astype(bf16)

    def finish(a, turn):
        flat = [jnp.sum(jnp.transpose(sums[turn, c]), axis=0, keepdims=True) for c in range(4)]
        both = dense_s[turn, :, 0:LANES] + dense_s[turn, :, LANES : 2 * LANES]
        flat = [flat[c] + (both[c : c + 1] + both[c + 4 : c + 5] + both[c + 8 : c + 9]) for c in range(4)]
        here = pl.ds(pl.multiple_of(a * LANES, LANES), LANES)
        for c in range(3):
            f_ref[c, :, here] = x_v[c, :, here] * flat[3] - flat[c]

    def force_block(a, turn):
        finish(lax.rem(a + blocks - 1, blocks), 1 - turn)
        dense_total = jnp.zeros((16, 2 * LANES), f32)
        for h in range(0, LANES, STRIP):
            share = dense * STRIP // LANES
            if share:
                here = slice(h // STRIP * share * LANES, (h // STRIP + 1) * share * LANES)
                dense_total = dense_total + jnp.dot(
                    left_s[turn, :, here], gt_v[a, here, :], preferred_element_type=f32
                )
            acc = [[jnp.zeros((8, LANES), f32) for _ in range(STRIP // 8)] for _ in range(4)]
            for k in range(listed - dense):
                rows = [
                    jnp.broadcast_to(coefs[turn, k * 4 + c : k * 4 + c + 1, :], (8, LANES)) for c in range(4)
                ]
                for q in range(STRIP // 8):
                    g = g_v[a * listed + k, h + q * 8 : h + q * 8 + 8, :]
                    for c in range(4):
                        acc[c][q] = acc[c][q] + g * rows[c]
            for c in range(4):
                for q in range(STRIP // 8):
                    sums[turn, c, h + q * 8 : h + q * 8 + 8, :] = acc[c][q]
        dense_s[turn] = dense_total
        ready(lax.rem(a + 1, blocks), 1 - turn)

    def forces(n, carry):
        force_block(2 * n, 0)
        force_block(2 * n + 1, 1)
        return carry

    ready(0, 0)
    sums[1] = jnp.zeros((4, LANES, LANES), f32)
    dense_s[1] = jnp.zeros((16, 2 * LANES), f32)
    lax.fori_loop(0, blocks // 2, forces, 0)
    finish(blocks - 1, 1)
    for n in range(1, replicas):
        mean_copy(n).wait_recv()
    messages = [mean_land[source[q]] for q in range(replicas)]
    for g in range(replicas):
        mean_ref[g * chunk : (g + 1) * chunk, :] = turned(messages, g)

    all_of(out_land, out_ss, out_rs).wait_send()
    all_of(back_land.at[0], back_ss, back_rs).wait_send()
    swap.wait_send()
    for n in range(chips):
        core_copy(n).wait_send()
    for s in range(1, domains):
        slot_copy(s).wait_send()
    for n in range(1, replicas):
        mean_copy(n).wait_send()


def hand_over(f_ref, mean_ref, f_out, mean_out):
    f_out[...] = f_ref[...]
    mean_out[...] = mean_ref[...]


def shards(
    coords, atom_var, atom_weight, atoms_live, block_list, owner_map,
    comp_means, comp_var, comp_weight, target, noise_sigma,
):
    replicas = lax.axis_size("rep")
    domains = lax.axis_size("dom")
    blocks, listed = block_list.shape
    comp_blocks = owner_map.shape[0]
    owned = target.shape[0] // LANES
    entries = blocks * listed
    slots = domains * CAPACITY
    chips = replicas // 2
    cells = chips * domains
    slab = CAPACITY // replicas
    per = LANES // CAPACITY
    dense = listed // 2 if slots == entries else listed // 4
    x = coords.transpose(1, 0, 2)
    cm = comp_means.reshape(3, comp_blocks, LANES).transpose(1, 0, 2)
    cv = comp_var.reshape(comp_blocks, 1, LANES)
    cw = comp_weight.reshape(comp_blocks, 1, LANES)
    whole = pl.BlockSpec(memory_space=VMEM)
    far = pl.BlockSpec(memory_space=pltpu.HBM)
    dma = pltpu.SemaphoreType.DMA
    forces, mean = pl.pallas_call(
        functools.partial(step_kernel, replicas, domains, blocks, listed, owned, dense),
        in_specs=[far] * 11,
        out_specs=[whole] * 2,
        out_shape=[
            jax.ShapeDtypeStruct(x.shape, f32),
            jax.ShapeDtypeStruct((owned, LANES), f32),
        ],
        scratch_shapes=[
            SMEM((blocks,), i32),
            SMEM((listed, blocks), i32),
            SMEM((comp_blocks,), i32),
            VMEM(x.shape, f32),
            VMEM((blocks, LANES), f32),
            VMEM((blocks, LANES), f32),
            VMEM((comp_blocks, 8, LANES), f32),
            VMEM((owned, LANES), f32),
            VMEM((owned, LANES), f32),
            VMEM((entries, LANES, LANES), f32),
            VMEM((2, 2 * LANES, ROWS), bf16),
            VMEM((2, LANES, LANES), f32),
            VMEM((2, 8 * listed, LANES), f32),
            VMEM((2, listed, LANES), f32),
            VMEM((2, listed // 2, 32, 2 * LANES), bf16),
            VMEM((entries, LANES), f32),
            VMEM((entries, LANES), i32),
            VMEM((slots, entries), bf16),
            VMEM((entries, slots), bf16),
            VMEM((slots // LANES, 8, LANES), f32),
            VMEM((domains, 8, LANES), f32),
            VMEM((replicas, domains, slab, LANES), f32),
            VMEM((chips, domains, slab, LANES), f32),
            VMEM((chips, domains, slab, LANES), f32),
            VMEM((cells, slab, LANES), f32),
            VMEM((domains, slab, LANES), f32),
            VMEM((2, cells, slab, LANES), f32),
            VMEM((domains, CAPACITY, LANES), f32),
            VMEM((entries, LANES), f32),
            VMEM((owned // replicas, LANES), f32),
            VMEM((replicas, owned // replicas, LANES), f32),
            VMEM((2, 4, LANES, LANES), f32),
            VMEM((2, 4 * (listed - dense), LANES), f32),
            VMEM((blocks, dense * LANES, 2 * LANES), bf16),
            VMEM((2, 16, dense * LANES), bf16),
            VMEM((2, 16, 2 * LANES), f32),
            VMEM((domains // per, LANES, owned), bf16),
            dma((11,)),
            dma((domains,)),
            dma((domains,)),
            dma((chips,)),
            dma((chips,)),
            dma,
            dma,
            dma,
            dma,
            dma,
            dma,
            dma((replicas,)),
            dma((replicas,)),
        ],
        compiler_params=pltpu.CompilerParams(
            collective_id=0, has_side_effects=True, vmem_limit_bytes=63 << 20
        ),
        name="step",
    )(
        atoms_live, block_list.T, owner_map, x,
        atom_var.reshape(blocks, LANES), atom_weight.reshape(blocks, LANES),
        cm, cv, cw, target.reshape(owned, LANES), noise_sigma.reshape(owned, LANES),
    )
    forces, mean = pl.pallas_call(
        hand_over,
        in_specs=[whole] * 2,
        out_specs=[whole] * 2,
        out_shape=[
            jax.ShapeDtypeStruct(x.shape, f32),
            jax.ShapeDtypeStruct((owned, LANES), f32),
        ],
        name="hand_over",
    )(forces, mean)
    return (mean.reshape(-1), forces.transpose(1, 0, 2))


def solution(mesh):
    return jax.shard_map(
        shards,
        mesh=mesh,
        in_specs=(
            P("rep", None, "dom"),
            P("dom"),
            P("dom"),
            P("dom"),
            P("dom", None),
            P(),
            P(),
            P(),
            P(),
            P("dom"),
            P("dom"),
        ),
        out_specs=(P("dom"), P("rep", None, "dom")),
        check_vma=False,
    )
```

```python
import functools
import math

import jax
import jax.numpy as jnp
from jax import lax
from jax.experimental import pallas as pl
from jax.experimental.pallas import tpu as pltpu
from jax.sharding import PartitionSpec as P

CAPACITY = 64
LANES = 128
STRIP = 32
ROWS = 64

energy_unit = 2.494
norm = (2.0 * math.pi) ** -1.5
half_log2e = -0.5 / math.log(2.0)
dead = -1.0e4
VMEM = pltpu.VMEM
SMEM = pltpu.SMEM
MESH = pl.DeviceIdType.MESH
f32, i32, bf16 = jnp.float32, jnp.int32, jnp.bfloat16


def split(value):
    second = value - value.astype(bf16).astype(f32)
    third = second - second.astype(bf16).astype(f32)
    return value, second, third


def pieces_of(value):
    return [piece.astype(bf16) for piece in split(value)]


def routed(picks, value):
    total = None
    for piece in pieces_of(value)[:2]:
        part = jnp.dot(picks, piece, preferred_element_type=f32)
        total = part if total is None else total + part
    return total


def iota(shape, axis):
    return lax.broadcasted_iota(i32, shape, axis)


def step_kernel(
    replicas, domains, blocks, listed, owned, dense,
    live_h, lst_h, owner_h, x_h, av_h, aw_h, m_h, cv_h, cw_h, target_h, sigma_h,
    f_ref, mean_ref,
    live, lst, owner, x_v, av_v, aw_v, table, target_v, sigma_v,
    g_v, lhs_s, avt_s, sum_s, cws, rhs_s, part, place_s, perm_a, perm_b, slot_send, slot_land,
    out_send, core_land, pair_send, out_land, back_send, back_land, ret, adj_e, mean_send, mean_land, sums, coefs, gt_v, left_s, dense_s, back_picks,
    loads, slot_ss, slot_rs, core_ss, core_rs, out_ss, out_rs, back_ss, back_rs, swap_ss, swap_rs, mean_ss, mean_rs,
):
    me_r = lax.axis_index("rep")
    me_d = lax.axis_index("dom")
    entries = blocks * listed
    slots = domains * CAPACITY
    width = LANES // replicas
    slab = CAPACITY // replicas
    per = LANES // CAPACITY
    chunk = owned // replicas
    chips = replicas // 2
    cells = chips * domains
    core = lax.rem(me_r, 2)
    fetches = [
        pltpu.make_async_copy(src, dst, loads.at[i])
        for i, (src, dst) in enumerate(
            [(lst_h, lst), (owner_h, owner), (live_h, live), (x_h, x_v), (av_h, av_v), (aw_h, aw_v),
             (m_h, table.at[:, 0:3, :]), (cv_h, table.at[:, 3:4, :]), (cw_h, table.at[:, 4:5, :]), (target_h, target_v), (sigma_h, sigma_v)]
        )
    ]
    for fetch in fetches:
        fetch.start()
    barrier = pltpu.get_barrier_semaphore()

    def pair_peer(n, sign):
        to_r = lax.rem(me_r + 2 * (n // domains), replicas)
        return to_r, lax.rem(me_d + domains + sign * lax.rem(n, domains), domains)

    def greet(n, carry):
        pl.semaphore_signal(barrier, inc=1, device_id=pair_peer(n, 1), device_id_type=MESH)
        return carry

    lax.fori_loop(1, cells, greet, 0)
    for n in range(1, replicas, 2):
        pl.semaphore_signal(
            barrier, inc=1, device_id=(lax.rem(me_r + n, replicas), me_d), device_id_type=MESH
        )
    for fetch in fetches[:6]:
        fetch.wait()

    lane = iota((1, LANES), 1)
    group = lane // width
    one = jnp.ones((1, LANES), f32)
    zero = jnp.zeros((1, LANES), f32)

    def places(a, carry):
        for k in range(listed):
            place_s[pl.ds(a * listed + k, 1), :] = jnp.full((1, LANES), owner[lst[k, a]], i32)
        return carry

    lax.fori_loop(0, blocks, places, 0)
    dev = lax.div(place_s[...], owned)
    slot = place_s[...] - dev * owned + 1
    hot = jnp.where(dev == lane, 1.0, 0.0)
    before = jnp.where(iota((entries, entries), 1) < iota((entries, entries), 0), 1.0, 0.0).astype(bf16)
    rank = jnp.dot(before, hot.astype(bf16), preferred_element_type=f32)
    rank = jnp.sum(rank * hot, axis=1, keepdims=True)
    place = dev * CAPACITY + jnp.broadcast_to(rank, (entries, LANES)).astype(i32)
    place_s[...] = place
    place_f = place.astype(f32)
    for j in range(entries // LANES):
        row = jnp.transpose(place_f[j * LANES : (j + 1) * LANES])[0:1].astype(i32)
        perm_a[:, j * LANES : (j + 1) * LANES] = jnp.where(
            iota((slots, LANES), 0) == row, 1.0, 0.0
        ).astype(bf16)
    slot_c = jnp.dot(perm_a[...], slot.astype(f32).astype(bf16), preferred_element_type=f32)
    for j in range(slots // LANES):
        slot_send[j] = jnp.transpose(slot_c[j * LANES : (j + 1) * LANES])[0:8]

    def slot_copy(s):
        to = lax.rem(me_d + s, domains)
        return pltpu.make_async_remote_copy(
            src_ref=slot_send.at[to // per], dst_ref=slot_land.at[s],
            send_sem=slot_ss.at[s], recv_sem=slot_rs.at[s],
            device_id=(me_r, to), device_id_type=MESH,
        )

    for fetch in fetches[6:]:
        fetch.wait()
    none = jnp.zeros((8, LANES), f32)
    row8 = iota((8, LANES), 0)
    fourth = jnp.where(row8 == 3, 1.0, 0.0)

    def last(value):
        return jnp.where(row8 == 7, jnp.broadcast_to(value, (8, LANES)), 0.0)

    def prepare(a, turn):
        x = jnp.concatenate(
            [x_v[c, :, pl.ds(pl.multiple_of(a * LANES, LANES), LANES)] for c in range(3)], axis=0
        )
        xx = jnp.sum(x * x, axis=0, keepdims=True)
        av = av_v[pl.ds(a, 1), :]
        lw = jnp.where(lane < live[a], jnp.log2(aw_v[pl.ds(a, 1), :]), dead)
        half = half_log2e * one
        left = jnp.concatenate([half_log2e * -2.0 * x, lw, half, half, half, half * xx + av * lw], axis=0)
        l0, l1, l2 = split(left)
        a0, a1, a2 = split(av)
        scaled_rows = jnp.concatenate([l0, l0, l1, l1, l0, l2, none, none], axis=0)
        width_rows = jnp.concatenate(
            [fourth + last(a0), fourth, last(a1), none, fourth, last(a2), none, none], axis=0
        )
        lhs_s[turn, 0:LANES] = jnp.transpose(scaled_rows.astype(bf16))
        lhs_s[turn, LANES : 2 * LANES] = jnp.transpose(width_rows.astype(bf16))
        avt_s[turn] = jnp.transpose(jnp.broadcast_to(av, (LANES, LANES)))
        for k in range(listed):
            tile = table[lst[k, a]]
            squares = pltpu.roll(tile * tile, 4, axis=0)
            r0, r1, r2 = split(jnp.where(row8 < 4, tile, jnp.where(row8 == 7, 1.0, squares)))
            here = slice((k % 2) * LANES, (k % 2 + 1) * LANES)
            rhs_s[turn, k // 2, 0:16, here] = jnp.concatenate([r0, r1], axis=0).astype(bf16)
            rhs_s[turn, k // 2, 16:32, here] = jnp.concatenate([r2, r0], axis=0).astype(bf16)

    def gather(a, turn):
        for h in range(0, listed, 8):
            total = sum_s[turn, pl.ds(h * 8, 8, stride=8), :]
            for r in range(1, 8):
                total = total + sum_s[turn, pl.ds(h * 8 + r, 8, stride=8), :]
            part[pl.ds(pl.multiple_of(a * listed + h, 8), 8), :] = total * (norm * cws[turn, h : h + 8, :])

    blank = jnp.zeros((16, 2 * LANES), bf16)

    def pair_block(a, turn):
        gather(lax.rem(a + blocks - 1, blocks), 1 - turn)
        for k in range(0, listed, 2):
            upper, lower = rhs_s[turn, k // 2, 0:16], rhs_s[turn, k // 2, 16:32]
            rhs = jnp.concatenate([upper, upper, lower, blank], axis=0)
            both = k % 8 == 0
            lhs = lhs_s[turn] if both else lhs_s[turn, 0:LANES]
            scaled = jnp.dot(lhs, rhs, preferred_element_type=f32)
            for i in range(2):
                e = a * listed + k + i
                b = lst[k + i, a]
                if not both:
                    cv = jnp.broadcast_to(table[b, 3:4, :], (8, LANES))
                total = jnp.zeros((8, LANES), f32)
                here = slice(i * LANES, (i + 1) * LANES)
                for h in range(0, LANES, 8):
                    if both:
                        root = lax.rsqrt(scaled[LANES + h : LANES + h + 8, here])
                    else:
                        root = lax.rsqrt(avt_s[turn, h : h + 8, :] + cv)
                    inv = root * root
                    ov = (root * inv) * jnp.exp2(scaled[h : h + 8, here] * inv)
                    total = total + ov
                    g_v[e, h : h + 8, :] = ov * inv
                sum_s[turn, (k + i) * 8 : (k + i) * 8 + 8, :] = total
                cws[turn, k + i : k + i + 1, :] = table[b, 4:5, :]
        prepare(lax.rem(a + 1, blocks), 1 - turn)

    def pairs(n, carry):
        pair_block(2 * n, 0)
        pair_block(2 * n + 1, 1)
        return carry

    sum_s[1] = jnp.zeros((8 * listed, LANES), f32)
    cws[1] = jnp.zeros((listed, LANES), f32)
    prepare(0, 0)
    early = blocks // 8
    lax.fori_loop(0, early, pairs, 0)
    pl.semaphore_wait(barrier, cells - 1 + chips)
    for s in range(1, domains):
        slot_copy(s).start()
    slot_land[0] = slot_send[me_d // per]
    lax.fori_loop(early, blocks // 2, pairs, 0)
    gather(blocks - 1, 1)

    def turned(pieces, to):
        total = None
        for g in range(replicas):
            shift = (width * (g - to)) % LANES
            piece = pltpu.roll(pieces[g], shift, axis=1) if shift else pieces[g]
            piece = jnp.where(group == g, piece, 0.0)
            total = piece if total is None else total + piece
        return total

    def fold(value):
        shift = width
        while shift < LANES:
            value = value + pltpu.roll(value, shift, axis=1)
            shift = 2 * shift
        return value

    placed = routed(perm_a[...], part[...]).reshape(domains, replicas, slab, LANES)
    parts = [placed[:, g].reshape(domains * slab, LANES) for g in range(replicas)]
    for q in range(replicas):
        out_send[q] = turned(parts, q).reshape(domains, slab, LANES)

    partner = (me_r + 1 - 2 * core, me_d)

    def core_copy(n):
        return pltpu.make_async_remote_copy(
            src_ref=out_send.at[2 * n + 1 - core], dst_ref=core_land.at[n],
            send_sem=core_ss.at[n], recv_sem=core_rs.at[n],
            device_id=partner, device_id_type=MESH,
        )

    def out_copy(n):
        to_r, to_d = pair_peer(n, 1)
        return pltpu.make_async_remote_copy(
            src_ref=pair_send.at[to_r // 2, to_d], dst_ref=out_land.at[n],
            send_sem=out_ss, recv_sem=out_rs,
            device_id=(to_r, to_d), device_id_type=MESH,
        )

    def all_of(land, send_sem, recv_sem):
        others = land.at[pl.ds(1, cells - 1)]
        return pltpu.make_async_remote_copy(
            src_ref=others, dst_ref=others, send_sem=send_sem, recv_sem=recv_sem,
            device_id=partner, device_id_type=MESH,
        )

    def start_out(n, carry):
        out_copy(cells - n).start()
        return carry

    for n in range(chips):
        core_copy(n).start()
    for n in range(chips):
        core_copy(n).wait_recv()
        pair_send[n] = out_send[2 * n + core] + core_land[n]
    lax.fori_loop(1, cells, start_out, 0)
    out_land[0] = pair_send[me_r // 2, me_d]

    def convert(a, carry):
        for k in range(dense):
            turned_g = jnp.transpose(g_v[a * listed + listed - dense + k])
            high = turned_g.astype(bf16)
            low = (turned_g - high.astype(f32)).astype(bf16)
            gt_v[a, k * LANES : (k + 1) * LANES, 0:LANES] = high
            gt_v[a, k * LANES : (k + 1) * LANES, LANES : 2 * LANES] = low
        return carry

    mine = group == me_r
    wanted = fold(jnp.where(mine, target_v[...], 0.0))
    sigmas = fold(jnp.where(mine, sigma_v[...], 0.0))
    for s in range(1, domains):
        slot_copy(s).wait_recv()
    odd = lax.rem(me_d, per)
    rows = []
    for j in range(domains // per):
        total = None
        for i in range(per):
            tile = slot_land[j * per + i]
            moved = None
            for n in range(per):
                shift = ((i - n) * CAPACITY) % LANES
                option = pltpu.roll(tile, shift, axis=1) if shift else tile
                moved = option if moved is None else jnp.where(odd == n, option, moved)
            moved = jnp.where(lane // CAPACITY == i, moved, 0.0)
            total = moved if total is None else total + moved
        rows.append(total[0:1])
    picks = jnp.concatenate(
        [jnp.where(iota((owned, LANES), 0) + 1 == row.astype(i32), 1.0, 0.0).astype(bf16) for row in rows],
        axis=1,
    )
    for j in range(domains // per):
        column = jnp.transpose(jnp.broadcast_to(rows[j], (LANES, LANES))).astype(i32)
        for i in range(max(1, owned // LANES)):
            span = min(owned, LANES)
            back_picks[j, :, i * span : (i + 1) * span] = jnp.where(
                column[:, :span] == iota((1, span), 1) + (i * span + 1), 1.0, 0.0
            ).astype(bf16)
    first_part = blocks // 2
    lax.fori_loop(0, first_part, convert, 0)

    all_of(out_land, out_ss, out_rs).wait_recv()
    spread = []
    for s in range(domains):
        total = out_land[s]
        for r in range(1, chips):
            total = total + out_land[r * domains + s]
        for g in range(replicas):
            spread.append(jnp.where(group == g, total, 0.0))
    mean = fold(routed(picks, jnp.concatenate(spread, axis=0))) / replicas
    misfit = mean - wanted
    adjoint = misfit / (sigmas * sigmas + 0.5 * misfit * misfit) / replicas
    adjoints = pieces_of(adjoint)[:2]
    for j in range(domains // per):
        value = None
        for piece in adjoints:
            part_j = jnp.dot(back_picks[j], piece, preferred_element_type=f32)
            value = part_j if value is None else value + part_j
        for i in range(per):
            packed = None
            for g in range(replicas):
                at = i * CAPACITY + g * slab
                piece = jnp.where(group == g, value[at : at + slab], 0.0)
                packed = piece if packed is None else packed + piece
            back_send[j * per + i] = packed

    def back_copy(n):
        return pltpu.make_async_remote_copy(
            src_ref=back_send.at[lax.rem(n, domains)], dst_ref=back_land.at[0, n],
            send_sem=back_ss, recv_sem=back_rs,
            device_id=pair_peer(n, -1), device_id_type=MESH,
        )

    def start_back(n, carry):
        back_copy(cells - n).start()
        return carry

    lax.fori_loop(1, cells, start_back, 0)
    back_land[0, 0] = back_send[0]
    packed = None
    for g in range(replicas):
        piece = jnp.where(group == g, mean[g * chunk : (g + 1) * chunk], 0.0)
        packed = piece if packed is None else packed + piece
    mean_send[...] = packed

    def mean_copy(n):
        return pltpu.make_async_remote_copy(
            src_ref=mean_send, dst_ref=mean_land.at[n],
            send_sem=mean_ss.at[n], recv_sem=mean_rs.at[n],
            device_id=(lax.rem(me_r + n, replicas), me_d), device_id_type=MESH,
        )

    for n in range(1, replicas):
        mean_copy(n).start()
    mean_land[0] = packed

    lax.fori_loop(first_part, blocks, convert, 0)
    for j in range(slots // LANES):
        perm_b[:, j * LANES : (j + 1) * LANES] = jnp.where(place_s[...] == lane + j * LANES, 1.0, 0.0).astype(bf16)

    for n in range(1, replicas):
        mean_copy(n).wait_recv()
    messages = [mean_land[lax.rem(me_r + replicas - q, replicas)] for q in range(replicas)]
    for g in range(replicas):
        mean_ref[g * chunk : (g + 1) * chunk, :] = turned(messages, g)

    all_of(back_land.at[0], back_ss, back_rs).wait_recv()
    swap = pltpu.make_async_remote_copy(
        src_ref=back_land.at[0], dst_ref=back_land.at[1], send_sem=swap_ss, recv_sem=swap_rs,
        device_id=partner, device_id_type=MESH,
    )
    swap.start()
    swap.wait_recv()
    for s in range(domains):
        messages = [
            back_land[lax.rem(core + q, 2), lax.rem(me_r // 2 + chips - q // 2, chips) * domains + s]
            for q in range(replicas)
        ]
        ret[lax.rem(me_d + s, domains)] = jnp.concatenate(
            [turned(messages, g) for g in range(replicas)], axis=0
        )
    adj_e[...] = routed(perm_b[...], ret[...].reshape(slots, LANES))
    def ready(a, turn):
        for k in range(listed):
            tile = table[lst[k, a]]
            scale = (energy_unit * norm) * tile[4:5] * adj_e[pl.ds(a * listed + k, 1), :]
            rows = (jnp.where(row8 == 3, 1.0, tile) * jnp.broadcast_to(scale, (8, LANES)))[0:4]
            if k < listed - dense:
                coefs[turn, k * 4 : k * 4 + 4, :] = rows
            else:
                at = k - listed + dense
                stack = jnp.concatenate([*split(rows), jnp.zeros((4, LANES), f32)], axis=0)
                left_s[turn, :, at * LANES : (at + 1) * LANES] = stack.astype(bf16)

    def finish(a, turn):
        flat = [jnp.sum(jnp.transpose(sums[turn, c]), axis=0, keepdims=True) for c in range(4)]
        both = dense_s[turn, :, 0:LANES] + dense_s[turn, :, LANES : 2 * LANES]
        flat = [flat[c] + (both[c : c + 1] + both[c + 4 : c + 5] + both[c + 8 : c + 9]) for c in range(4)]
        here = pl.ds(pl.multiple_of(a * LANES, LANES), LANES)
        for c in range(3):
            f_ref[c, :, here] = x_v[c, :, here] * flat[3] - flat[c]

    def force_block(a, turn):
        finish(lax.rem(a + blocks - 1, blocks), 1 - turn)
        dense_total = jnp.zeros((16, 2 * LANES), f32)
        for h in range(0, LANES, STRIP):
            share = dense * STRIP // LANES
            if share:
                here = slice(h // STRIP * share * LANES, (h // STRIP + 1) * share * LANES)
                dense_total = dense_total + jnp.dot(
                    left_s[turn, :, here], gt_v[a, here, :], preferred_element_type=f32
                )
            acc = [[jnp.zeros((8, LANES), f32) for _ in range(STRIP // 8)] for _ in range(4)]
            for k in range(listed - dense):
                rows = [
                    jnp.broadcast_to(coefs[turn, k * 4 + c : k * 4 + c + 1, :], (8, LANES)) for c in range(4)
                ]
                for q in range(STRIP // 8):
                    g = g_v[a * listed + k, h + q * 8 : h + q * 8 + 8, :]
                    for c in range(4):
                        acc[c][q] = acc[c][q] + g * rows[c]
            for c in range(4):
                for q in range(STRIP // 8):
                    sums[turn, c, h + q * 8 : h + q * 8 + 8, :] = acc[c][q]
        dense_s[turn] = dense_total
        ready(lax.rem(a + 1, blocks), 1 - turn)

    def forces(n, carry):
        force_block(2 * n, 0)
        force_block(2 * n + 1, 1)
        return carry

    ready(0, 0)
    sums[1] = jnp.zeros((4, LANES, LANES), f32)
    dense_s[1] = jnp.zeros((16, 2 * LANES), f32)
    lax.fori_loop(0, blocks // 2, forces, 0)
    finish(blocks - 1, 1)
    all_of(out_land, out_ss, out_rs).wait_send()
    all_of(back_land.at[0], back_ss, back_rs).wait_send()
    swap.wait_send()
    for n in range(chips):
        core_copy(n).wait_send()
    for s in range(1, domains):
        slot_copy(s).wait_send()
    for n in range(1, replicas):
        mean_copy(n).wait_send()


def hand_over(f_ref, mean_ref, f_out, mean_out):
    f_out[...] = f_ref[...]
    mean_out[...] = mean_ref[...]


def shards(
    coords, atom_var, atom_weight, atoms_live, block_list, owner_map,
    comp_means, comp_var, comp_weight, target, noise_sigma,
):
    replicas = lax.axis_size("rep")
    domains = lax.axis_size("dom")
    blocks, listed = block_list.shape
    comp_blocks = owner_map.shape[0]
    owned = target.shape[0] // LANES
    entries = blocks * listed
    slots = domains * CAPACITY
    chips = replicas // 2
    cells = chips * domains
    slab = CAPACITY // replicas
    per = LANES // CAPACITY
    dense = listed // 2 if slots == entries else listed // 4
    x = coords.transpose(1, 0, 2)
    cm = comp_means.reshape(3, comp_blocks, LANES).transpose(1, 0, 2)
    cv = comp_var.reshape(comp_blocks, 1, LANES)
    cw = comp_weight.reshape(comp_blocks, 1, LANES)
    whole = pl.BlockSpec(memory_space=VMEM)
    far = pl.BlockSpec(memory_space=pltpu.HBM)
    dma = pltpu.SemaphoreType.DMA
    forces, mean = pl.pallas_call(
        functools.partial(step_kernel, replicas, domains, blocks, listed, owned, dense),
        in_specs=[far] * 11,
        out_specs=[whole] * 2,
        out_shape=[
            jax.ShapeDtypeStruct(x.shape, f32),
            jax.ShapeDtypeStruct((owned, LANES), f32),
        ],
        scratch_shapes=[
            SMEM((blocks,), i32),
            SMEM((listed, blocks), i32),
            SMEM((comp_blocks,), i32),
            VMEM(x.shape, f32),
            VMEM((blocks, LANES), f32),
            VMEM((blocks, LANES), f32),
            VMEM((comp_blocks, 8, LANES), f32),
            VMEM((owned, LANES), f32),
            VMEM((owned, LANES), f32),
            VMEM((entries, LANES, LANES), f32),
            VMEM((2, 2 * LANES, ROWS), bf16),
            VMEM((2, LANES, LANES), f32),
            VMEM((2, 8 * listed, LANES), f32),
            VMEM((2, listed, LANES), f32),
            VMEM((2, listed // 2, 32, 2 * LANES), bf16),
            VMEM((entries, LANES), f32),
            VMEM((entries, LANES), i32),
            VMEM((slots, entries), bf16),
            VMEM((entries, slots), bf16),
            VMEM((slots // LANES, 8, LANES), f32),
            VMEM((domains, 8, LANES), f32),
            VMEM((replicas, domains, slab, LANES), f32),
            VMEM((chips, domains, slab, LANES), f32),
            VMEM((chips, domains, slab, LANES), f32),
            VMEM((cells, slab, LANES), f32),
            VMEM((domains, slab, LANES), f32),
            VMEM((2, cells, slab, LANES), f32),
            VMEM((domains, CAPACITY, LANES), f32),
            VMEM((entries, LANES), f32),
            VMEM((owned // replicas, LANES), f32),
            VMEM((replicas, owned // replicas, LANES), f32),
            VMEM((2, 4, LANES, LANES), f32),
            VMEM((2, 4 * (listed - dense), LANES), f32),
            VMEM((blocks, dense * LANES, 2 * LANES), bf16),
            VMEM((2, 16, dense * LANES), bf16),
            VMEM((2, 16, 2 * LANES), f32),
            VMEM((domains // per, LANES, owned), bf16),
            dma((11,)),
            dma((domains,)),
            dma((domains,)),
            dma((chips,)),
            dma((chips,)),
            dma,
            dma,
            dma,
            dma,
            dma,
            dma,
            dma((replicas,)),
            dma((replicas,)),
        ],
        compiler_params=pltpu.CompilerParams(
            collective_id=0, has_side_effects=True, vmem_limit_bytes=63 << 20
        ),
        name="step",
    )(
        atoms_live, block_list.T, owner_map, x,
        atom_var.reshape(blocks, LANES), atom_weight.reshape(blocks, LANES),
        cm, cv, cw, target.reshape(owned, LANES), noise_sigma.reshape(owned, LANES),
    )
    forces, mean = pl.pallas_call(
        hand_over,
        in_specs=[whole] * 2,
        out_specs=[whole] * 2,
        out_shape=[
            jax.ShapeDtypeStruct(x.shape, f32),
            jax.ShapeDtypeStruct((owned, LANES), f32),
        ],
        name="hand_over",
    )(forces, mean)
    return (mean.reshape(-1), forces.transpose(1, 0, 2))


def solution(mesh):
    return jax.shard_map(
        shards,
        mesh=mesh,
        in_specs=(
            P("rep", None, "dom"),
            P("dom"),
            P("dom"),
            P("dom"),
            P("dom", None),
            P(),
            P(),
            P(),
            P(),
            P("dom"),
            P("dom"),
        ),
        out_specs=(P("dom"), P("rep", None, "dom")),
        check_vma=False,
    )
```
